32 devices in a mesh: req: 16 (over z, y, core), tp: 2 (over x).
Axes of the slice: x: 2, y: 2, z: 4, core: 2. Of those that a mesh axis runs over, the one named last changes fastest.
Arguments:
- tokens: bfloat16 [4096, 2048], P(('req', 'tp')), may hold values from -6 to 6
- norm_gain: float32 [2048], replicated, may hold values from 0.1 to 1.9
- w_query: bfloat16 [2048, 2048], P('req', 'tp'), may hold values from -0.375 to 0.375
- w_kv: bfloat16 [2048, 8, 128], P('req', 'tp'), may hold values from -5 to 5
- w_out: bfloat16 [2048, 2048], P('tp', 'req'), may hold values from -0.125 to 0.125
- kv_cache: bfloat16 [1024, 128, 8, 128], P('req', None, 'tp'), may hold values from -280 to 280
- page_table: int32 [16, 64], P('req'), may hold values from 0 to 63, as said below
- cached_len: int32 [16], replicated, may hold values from 0 to 8192, as said below
- span_len: int32 [16], P('req'), may hold values from 1 to 256, as said below
Outputs:
- update: bfloat16 [4096, 2048], P(('req', 'tp'))
The draws below stay inside these ranges and needn't reach their ends.
Inputs may be any that keep to these rules, and one draw needn't show every extreme that they name: `page_table`: each row lists pages of the pool block of the request's req index; the 1 row of one index together hold every page of that block exactly once. `cached_len`: some request has 8192 cached tokens and some has none. Tokens from span_len on are padding; some span is full and some holds one token.
All inputs are finite; a program needn't handle non-finite values.
Results may differ from the reference program's by a relative error of at most 0.02.
The reference program's roundings to bfloat16 on the way (of `normed`, `query_rot`, `new_keys`, `new_values`, `weights`, `attended` and `piece_term`) count: a program that leaves them out, or rounds other values in their place, can miss the bound.
Values may be sent and summed in bfloat16 or wider, within the bound.
No kernel may reach another device: no remote copies, remote signals or barrier semaphores. Data moves between devices by JAX's collectives and lax.ppermute only.
A program may use at most 128 MiB of HBM per device.

```python
import math
import jax
import jax.numpy as jnp
from jax import lax

D = 2048
H = 32
KVH = 8
HD = 64
SPAN = 256
PAGE = 128
MAXPAGES = 64
REQ_DEV = 1
MAXLEN = 8192
POOL_DEV = 64
PAGES = 1024
REQS = 16
TOKENS = 4096
N_TP = 2


def draw_w_kv(key, part):
    shape = (D, KVH, 2 * HD)
    column = jnp.arange(2 * HD)
    factor = jnp.where(column < HD, 8.0, 1.0) / math.sqrt(D)
    base = jnp.clip(jax.random.normal(key, shape, jnp.float32), -5.0, 5.0)
    return (base * factor).astype(jnp.bfloat16)


def draw_kv_cache(key, part):
    shape = (PAGES, PAGE, KVH, 2 * HD)
    column = jnp.arange(2 * HD)
    base = jnp.clip(jax.random.normal(key, shape, jnp.float32), -5.0, 5.0)
    key_part = 8.0 * base
    value_part = base
    return jnp.where(column < HD, key_part, value_part).astype(jnp.bfloat16)


def draw_page_table(key, part):
    devices = REQS // REQ_DEV
    keys = jax.random.split(key, devices)
    perms = jax.vmap(lambda single: jax.random.permutation(single, POOL_DEV))(keys)
    return perms.reshape(REQS, MAXPAGES).astype(jnp.int32)


def draw_cached_len(key, part):
    keys = jax.random.split(jax.random.fold_in(key, 7), 4)
    longs = jax.random.randint(keys[0], (REQS,), 0, 2)
    short = jax.random.randint(keys[1], (REQS,), 0, MAXLEN // 8 + 1)
    near = MAXLEN - jax.random.randint(keys[2], (REQS,), 0, MAXLEN // 8)
    lengths = jnp.where(longs == 1, near, short)
    order = jax.random.permutation(keys[3], REQS)
    slots = jnp.arange(REQS)
    lengths = jnp.where(slots == order[0], MAXLEN, jnp.where(slots == order[1], 0, lengths))
    return lengths.astype(jnp.int32)


def draw_span_len(key, part):
    keys = jax.random.split(jax.random.fold_in(key, 11), 2)
    lengths = jax.random.randint(keys[0], (REQS,), 1, SPAN + 1)
    order = jax.random.permutation(keys[1], REQS)
    slots = jnp.arange(REQS)
    lengths = jnp.where(slots == order[0], SPAN, jnp.where(slots == order[1], 1, lengths))
    return lengths.astype(jnp.int32)


def shard_levels(own_key, shape, pieces, least, high):
    factor_of, own = 1.0, jax.random.fold_in(own_key, 6)
    for dim, shards_of in pieces:
        heights = jnp.exp(jax.random.uniform(jax.random.fold_in(own, dim), (shards_of,), jnp.float32, least / len(pieces), high / len(pieces)))
        factor_of = factor_of * jnp.repeat(heights, shape[dim] // shards_of).reshape([-1 if axis == dim else 1 for axis in range(len(shape))])
    return factor_of


def normal_values(rng, shape, spread, most, pieces=(), held_as=jnp.bfloat16):
    drawn = jax.random.normal(rng, shape, jnp.float32) * spread
    if len(pieces) > 0:
        drawn = shard_levels(rng, shape, pieces, -0.22, 0.18) * drawn
    return jnp.clip(drawn, min=-most, max=most).astype(held_as)


def setup_inputs(seed: int = 0) -> dict:
    seeds = jax.random.split(jax.random.key(seed), 10)
    tokens = normal_values(seeds[0], (TOKENS, D), 1.0, 6.0, ((0, 32),))
    norm_gain = jnp.clip(1.0 + 0.18 * jax.random.normal(seeds[1], (D,), jnp.float32), 0.1, 1.9)
    w_query = normal_values(seeds[2], (D, H * HD), (D // 9) ** -0.5, 0.375, ((0, 16), (1, 2)))
    w_kv = draw_w_kv(jax.random.fold_in(seeds[9], 71), 0)
    w_out = normal_values(seeds[4], (H * HD, D), (H * HD) ** -0.5, 0.125, ((0, 2), (1, 16)))
    kv_cache = draw_kv_cache(jax.random.fold_in(seeds[9], 71), 0)
    page_table = draw_page_table(jax.random.fold_in(seeds[9], 71), 0)
    cached_len = draw_cached_len(jax.random.fold_in(seeds[9], 71), 0)
    span_len = draw_span_len(jax.random.fold_in(seeds[9], 71), 0)
    return {"tokens": tokens, "norm_gain": norm_gain, "w_query": w_query, "w_kv": w_kv, "w_out": w_out, "kv_cache": kv_cache, "page_table": page_table, "cached_len": cached_len, "span_len": span_len}


epsilon = 1e-05
score_scale = 0.015625
residual_scale = 0.22
rope_base = 10000000.0
masked_score = -1e+30

def rotate(values, positions):
    half_dim = values.shape[-1] // 2
    frequency = rope_base ** (-(jnp.arange(half_dim, dtype=jnp.float32) * 2.0 / values.shape[-1]))
    angles = positions.astype(jnp.float32)[:, None, None] * frequency[None, None, :]
    cosine = jnp.cos(angles)
    sines = jnp.sin(angles)
    first_half = values[..., :half_dim]
    second = values[..., half_dim:]
    return jnp.concatenate([first_half * cosine - second * sines, second * cosine + first_half * sines], axis=-1)

def reference(tokens, norm_gain, w_query, w_kv, w_out, kv_cache, page_table, cached_len, span_len):
    hidden = tokens.astype(jnp.float32)
    normed = (hidden * lax.rsqrt(lax.optimization_barrier(jnp.mean(hidden * hidden, axis=-1, keepdims=True)) + epsilon) * norm_gain).astype(jnp.bfloat16)
    projected = jnp.dot(normed, w_query, preferred_element_type=jnp.float32).reshape(REQS, SPAN, H, HD)
    key_value = jnp.dot(normed, w_kv.reshape(D, KVH * 2 * HD), preferred_element_type=jnp.float32).reshape(REQS, SPAN, KVH, 2 * HD)
    offsets = jnp.arange(SPAN, dtype=jnp.int32)
    cache_slots = jnp.arange(MAXPAGES * PAGE, dtype=jnp.int32)
    causal = offsets[None, :] <= offsets[:, None]
    owners = jnp.arange(REQS, dtype=jnp.int32) // REQ_DEV * POOL_DEV

    def one_request(inputs):
        query_block, pair_block, table_row, owner_base, length, valid_len = inputs
        positions = length + offsets
        query_rot = lax.optimization_barrier(rotate(query_block, positions).astype(jnp.bfloat16))
        new_keys = lax.optimization_barrier(rotate(pair_block[..., :HD], positions).astype(jnp.bfloat16))
        new_values = lax.optimization_barrier(pair_block[..., HD:].astype(jnp.bfloat16))
        pages = jnp.take(kv_cache, (table_row + owner_base).astype(jnp.int32), axis=0).reshape(MAXPAGES * PAGE, KVH, 2 * HD)
        all_keys = jnp.concatenate([pages[..., :HD], new_keys], axis=0).astype(jnp.float32)
        all_values = jnp.concatenate([pages[..., HD:], new_values], axis=0).astype(jnp.float32)
        cache_ok = jnp.broadcast_to((cache_slots < length)[None, :], (SPAN, MAXPAGES * PAGE))
        span_ok = causal & (offsets[None, :] < valid_len)
        allowed = jnp.concatenate([cache_ok, span_ok], axis=1)
        grouped = query_rot.astype(jnp.float32).reshape(SPAN, KVH, H // KVH, HD)
        scores = score_scale * jnp.einsum('tkgd,skd->kgts', grouped, all_keys)
        scores = jnp.where(allowed[None, None], scores, masked_score)
        maximum = lax.optimization_barrier(jnp.max(scores, axis=-1, keepdims=True))
        exponent = jnp.where(allowed[None, None], jnp.exp(scores - maximum), 0.0)
        running = lax.optimization_barrier(jnp.sum(exponent, axis=-1))
        weights = lax.optimization_barrier(exponent.astype(jnp.bfloat16)).astype(jnp.float32)
        mixed = jnp.einsum('kgts,skd->tkgd', weights, all_values) / jnp.transpose(running, (2, 0, 1))[..., None]
        mixed = jnp.where((offsets < valid_len)[:, None, None, None], mixed, 0.0)
        return mixed.reshape(SPAN, H * HD).astype(jnp.bfloat16)
    attended = lax.map(one_request, (projected, key_value, page_table, owners, cached_len, span_len))
    attended = attended.reshape(REQS * SPAN, H * HD)
    group_width = H * HD // N_TP
    summed = jnp.zeros((REQS * SPAN, D), jnp.float32)
    for part_index in range(N_TP):
        lower = part_index * group_width
        piece_term = jnp.dot(attended[:, lower:lower + group_width], w_out[lower:lower + group_width], preferred_element_type=jnp.float32)
        summed = summed + lax.optimization_barrier(piece_term.astype(jnp.bfloat16)).astype(jnp.float32)
    return (residual_scale * summed).astype(jnp.bfloat16)
```

```python
import functools

import jax
import jax.numpy as jnp
from jax import lax
from jax.experimental import pallas as pl
from jax.experimental.pallas import tpu as pltpu
from jax.sharding import PartitionSpec as P

epsilon = 1e-05
score_scale = 0.015625
residual_scale = 0.22
rope_base = 10000000.0
masked_score = -1e30
key_block = 1024
score_chunk = 256
value_chunk = 256
token_tile = 128
vmem_limit = 60 * 1024 * 1024


def matmul(a, b):
    return jnp.dot(a, b, preferred_element_type=jnp.float32)


def vmem():
    return pl.BlockSpec(memory_space=pltpu.VMEM)


def smem():
    return pl.BlockSpec(memory_space=pltpu.SMEM)


def params():
    return pltpu.CompilerParams(vmem_limit_bytes=vmem_limit)


def cycle_tables(count):
    depth = count // 4
    walk = [(z, 0) for z in range(depth)] + [(z, 1) for z in reversed(range(depth))]
    device = lambda chip, core: (chip[0] * 2 + chip[1]) * 2 + core
    length = len(walk)
    ahead = [
        (device(walk[k], c), device(walk[(k + 1) % length], c))
        for k in range(length)
        for c in range(2)
    ]
    back = [(b, a) for a, b in ahead]
    swap = [(i, i ^ 1) for i in range(count)]
    order = [None] * count
    for k in range(length):
        for c in range(2):
            row = []
            for step in range(length // 2):
                sources = [walk[(k - step) % length], walk[(k + step) % length]]
                for chip in sources[: 1 if step == 0 else 2]:
                    row += [device(chip, c), device(chip, 1 - c)]
            far = walk[(k + length // 2) % length]
            row += [device(far, c), device(far, 1 - c)]
            order[device(walk[k], c)] = row
    return ahead, back, swap, order


def ring_gather(shard, tables, after=None):
    ahead, back, swap, order = tables
    move = lambda value, pairs: lax.ppermute(value, "req", pairs)
    length = len(order) // 2
    half = shard.shape[0] // 2
    blocks = [shard, move(shard, swap)]
    up = down = shard
    for _ in range(length // 2 - 1):
        up, down = move(up, ahead), move(down, back)
        blocks += [up, move(up, swap), down, move(down, swap)]
    first, second = move(up[:half], ahead), move(down[half:], back)
    return blocks, [first, second, move(first, swap), move(second, swap)]


def prepare_kernel(heads, page, width, pages_step, table_ref, length_ref, *refs):
    pages = refs[:pages_step]
    key_ref, value_ref, wide = refs[pages_step:]
    step = pl.program_id(0)
    half = width // 2
    for i in range(pages_step):
        wide[...] = pages[i][0].astype(jnp.float32)
        first = (step * pages_step + i) * page
        position = first + lax.broadcasted_iota(jnp.int32, (page, width), 0)
        lane = lax.broadcasted_iota(jnp.int32, (page, width), 1)
        bias = jnp.where((lane == half) & (position >= length_ref[0]), masked_score, 0.0)
        for h in range(heads):
            rows = wide[pl.ds(h, page, stride=heads), :]
            key_ref[h, pl.ds(i * page, page), :] = jnp.where(lane < half, rows, bias).astype(
                jnp.bfloat16
            )
            turned = jnp.transpose(rows)[half:]
            value_ref[h, :, pl.ds(i * page, page)] = with_ones(turned).astype(jnp.bfloat16)


def with_ones(turned):
    row = lax.broadcasted_iota(jnp.int32, (16, turned.shape[1]), 0)
    return jnp.concatenate([turned, jnp.where(row == 0, 1.0, 0.0)], axis=0)


def prepare(cache, table, length):
    pages, page, heads, width = cache.shape
    pages_step = 4
    rows = width // 2 + 16
    flat = cache.reshape(pages, page * heads, width)
    page_spec = lambda i: pl.BlockSpec(
        (1, page * heads, width), lambda j, t, n: (t[j * pages_step + i], 0, 0)
    )
    return pl.pallas_call(
        functools.partial(prepare_kernel, heads, page, width, pages_step),
        grid_spec=pltpu.PrefetchScalarGridSpec(
            num_scalar_prefetch=2,
            grid=(table.shape[0] // pages_step,),
            in_specs=[page_spec(i) for i in range(pages_step)],
            out_specs=[
                pl.BlockSpec((heads, pages_step * page, width), lambda j, t, n: (0, j, 0)),
                pl.BlockSpec((heads, rows, pages_step * page), lambda j, t, n: (0, 0, j)),
            ],
            scratch_shapes=[pltpu.VMEM((page * heads, width), jnp.float32)],
        ),
        out_shape=[
            jax.ShapeDtypeStruct((heads, table.shape[0] * page, width), jnp.bfloat16),
            jax.ShapeDtypeStruct((heads, rows, table.shape[0] * page), jnp.bfloat16),
        ],
        cost_estimate=pl.CostEstimate(
            flops=0, bytes_accessed=4 * cache.size * cache.dtype.itemsize, transcendentals=0
        ),
        compiler_params=params(),
        name="prepare",
    )(table, length, *([flat] * pages_step))


def turn(pair, cosine, sines):
    half = pair.shape[0] // 2
    first, second = pair[:half], pair[half:]
    return jnp.concatenate(
        [first * cosine - second * sines, second * cosine + first * sines], axis=0
    )


def project_kernel(heads, group, dim, blocks, order_ref, *refs):
    chunks = refs[:blocks]
    normed_ref, cos_ref, sin_ref, query_ref, key_ref, value_ref, weight = refs[blocks:]
    rows = weight.shape[0] // order_ref.shape[0]
    if blocks == 1:
        source = chunks[0]
    else:
        source = weight
        for k in range(order_ref.shape[0]):
            start = pl.multiple_of(order_ref[k] * rows, rows)
            if k < order_ref.shape[0] - 2:
                weight[pl.ds(start, rows), :] = chunks[k][...]
            else:
                at = order_ref.shape[0] - 2 + 2 * (k - (order_ref.shape[0] - 2))
                weight[pl.ds(start, rows), :] = jnp.concatenate(
                    [chunks[at][...], chunks[at + 1][...]], axis=0
                )
    cosine, sines = cos_ref[...], sin_ref[...]
    tokens = cosine.shape[1]
    normed = normed_ref[...]
    width = group * dim
    for h in range(heads):
        turned = jnp.transpose(matmul(normed, source[:, pl.ds(h * width, width)]))
        for g in range(group):
            rotated = turn(turned[g * dim : (g + 1) * dim], cosine, sines).astype(jnp.bfloat16)
            scaled = (rotated.astype(jnp.float32) * score_scale).astype(jnp.bfloat16)
            for q in range(tokens // token_tile):
                query_ref[h, q, pl.ds(0, dim), pl.ds(g * token_tile, token_tile)] = scaled[
                    :, q * token_tile : (q + 1) * token_tile
                ]
        row = lax.broadcasted_iota(jnp.int32, (dim, group * token_tile), 0)
        for q in range(tokens // token_tile):
            query_ref[h, q, pl.ds(dim, dim), :] = jnp.where(row == 0, 1.0, 0.0).astype(jnp.bfloat16)
    for h in range(heads):
        at = heads * width + h * 2 * dim
        turned = jnp.transpose(matmul(normed, source[:, pl.ds(at, 2 * dim)]))
        keys = turn(turned[:dim], cosine, sines)
        padded = jnp.concatenate([keys, jnp.zeros_like(keys)], axis=0)
        key_ref[h] = jnp.transpose(padded).astype(jnp.bfloat16)
        value_ref[h] = with_ones(turned[dim:]).astype(jnp.bfloat16)


def project(normed, chunks, order, cosine, sines, heads, group, dim):
    tokens, width = normed.shape
    columns = chunks[0].shape[1]
    return pl.pallas_call(
        functools.partial(project_kernel, heads, group, dim, len(chunks)),
        in_specs=[smem()] + [vmem()] * (len(chunks) + 3),
        out_specs=[vmem()] * 3,
        out_shape=[
            jax.ShapeDtypeStruct(
                (heads, tokens // token_tile, 2 * dim, group * token_tile), jnp.bfloat16
            ),
            jax.ShapeDtypeStruct((heads, tokens, 2 * dim), jnp.bfloat16),
            jax.ShapeDtypeStruct((heads, dim + 16, tokens), jnp.bfloat16),
        ],
        scratch_shapes=[pltpu.VMEM((width, columns), jnp.bfloat16)],
        cost_estimate=pl.CostEstimate(
            flops=2 * tokens * width * columns,
            bytes_accessed=2 * width * columns,
            transcendentals=0,
        ),
        compiler_params=params(),
        name="project",
    )(order, *chunks, normed, cosine, sines)


def attend_kernel(
    group,
    dim,
    length_ref,
    span_ref,
    key_ref,
    value_ref,
    query_ref,
    new_key_ref,
    new_value_ref,
    out_ref,
    even,
    odd,
):
    lanes = query_ref.shape[3]
    span = new_key_ref.shape[1]
    length = length_ref[0]
    valid = span_ref[0]
    pair = 2 * key_block
    pairs = (length + pair - 1) // pair
    last_block = jnp.maximum(2 * pairs - 1, 0)

    def column_max(scores):
        return jnp.max(scores.reshape(scores.shape[0] // 8, 8, lanes), axis=0)

    def tile(q, _):
        def scores_of(block, c, target):
            start = pl.multiple_of(block * key_block + c * score_chunk, score_chunk)
            scores = matmul(key_ref[0, pl.ds(start, score_chunk), :], query_ref[0, q])
            target[pl.ds(c * score_chunk, score_chunk), :] = scores
            return column_max(scores)

        scores = matmul(new_key_ref[0], query_ref[0, q])
        source = lax.broadcasted_iota(jnp.int32, (span, lanes), 0)
        lane = lax.broadcasted_iota(jnp.int32, (span, lanes), 1)
        token = q * token_tile + lax.rem(lane, token_tile)
        scores = jnp.where((source <= token) & (source < valid), scores, masked_score)
        maximum = jnp.max(column_max(scores), axis=0, keepdims=True)
        weights = jnp.exp(scores - maximum).astype(jnp.bfloat16)
        total = matmul(new_value_ref[0], weights)

        top = scores_of(0, 0, even)
        for c in range(1, key_block // score_chunk):
            top = jnp.maximum(top, scores_of(0, c, even))

        def half(block, following, current, target, state):
            maximum, top, total = state
            new_maximum = jnp.maximum(maximum, jnp.max(top, axis=0, keepdims=True))
            total = total * jnp.exp(maximum - new_maximum)
            next_top = None
            ratio = value_chunk // score_chunk
            parts = []
            for c in range(key_block // score_chunk):
                seen = scores_of(following, c, target)
                next_top = seen if next_top is None else jnp.maximum(next_top, seen)
                part = jnp.exp(current[pl.ds(c * score_chunk, score_chunk), :] - new_maximum)
                parts.append(part.astype(jnp.bfloat16))
                if len(parts) == ratio:
                    weights = parts[0] if ratio == 1 else jnp.concatenate(parts, axis=0)
                    start = block * key_block + (c + 1 - ratio) * score_chunk
                    start = pl.multiple_of(start, value_chunk)
                    total = total + matmul(value_ref[0, :, pl.ds(start, value_chunk)], weights)
                    parts = []
            return new_maximum, next_top, total

        def advance(i, state):
            block = 2 * i
            state = half(block, block + 1, even, odd, state)
            following = jnp.minimum(block + 2, last_block)
            return half(block + 1, following, odd, even, state)

        _, _, total = lax.fori_loop(0, pairs, advance, (maximum, top, total))
        result = total[:dim] / total[dim : dim + 1]
        row = q * token_tile + lax.broadcasted_iota(jnp.int32, (token_tile, 2 * dim), 0)
        for g in range(0, group, 2):
            both = jnp.concatenate(
                [
                    result[:, g * token_tile : (g + 1) * token_tile],
                    result[:, (g + 1) * token_tile : (g + 2) * token_tile],
                ],
                axis=0,
            )
            kept = jnp.where(row < valid, jnp.transpose(both), 0.0)
            out_ref[pl.ds(pl.multiple_of(q * token_tile, token_tile), token_tile), pl.ds(g * dim, 2 * dim)] = (
                kept.astype(jnp.bfloat16)
            )
        return 0

    tiles = (valid + token_tile - 1) // token_tile
    out_ref[...] = jnp.zeros_like(out_ref)
    lax.fori_loop(0, tiles, tile, 0)


def attend(head, keys, values, queries, new_keys, new_values, length, valid):
    _, cached, width = keys.shape
    dim = width // 2
    _, tiles, _, lanes = queries.shape
    group = lanes // token_tile
    tokens = tiles * token_tile
    block = lambda array: pl.BlockSpec(
        (1,) + array.shape[1:], lambda i: (head,) + (0,) * (array.ndim - 1)
    )
    arrays = (keys, values, queries, new_keys, new_values)
    return pl.pallas_call(
        functools.partial(attend_kernel, group, dim),
        grid=(1,),
        in_specs=[smem(), smem()] + [block(a) for a in arrays],
        out_specs=pl.BlockSpec((tokens, group * dim), lambda i: (0, 0)),
        out_shape=jax.ShapeDtypeStruct((tokens, group * dim), jnp.bfloat16),
        scratch_shapes=[pltpu.VMEM((key_block, lanes), jnp.float32)] * 2,
        cost_estimate=pl.CostEstimate(
            flops=2 * cached * tokens * group * 2 * width,
            bytes_accessed=2 * cached * 2 * width,
            transcendentals=cached * tokens * group,
        ),
        compiler_params=params(),
        name="attend",
    )(length, valid, *arrays)


def emit_kernel(heads, blocks, start_ref, *refs):
    parts = refs[:heads]
    chunks = refs[heads : heads + blocks]
    out_ref = refs[heads + blocks]
    rows = out_ref.shape[1]
    start = pl.multiple_of(start_ref[0], rows)
    attended = jnp.concatenate([p[pl.ds(start, rows), :] for p in parts], axis=1)
    count = out_ref.shape[0]
    for k in range(0, count, 2):
        if k < count - 2:
            weight = jnp.concatenate([chunks[k][...], chunks[k + 1][...]], axis=1)
        else:
            at = count - 2
            own = jnp.concatenate([chunks[at][...], chunks[at + 1][...]], axis=0)
            other = jnp.concatenate([chunks[at + 2][...], chunks[at + 3][...]], axis=0)
            weight = jnp.concatenate([own, other], axis=1)
        both = matmul(attended, weight).astype(jnp.bfloat16)
        width = both.shape[1] // 2
        out_ref[k] = both[:, :width]
        out_ref[k + 1] = both[:, width:]


def emit(parts, chunks, start, rows, count):
    columns = chunks[0].shape[1]
    depth = chunks[0].shape[0]
    return pl.pallas_call(
        functools.partial(emit_kernel, len(parts), len(chunks)),
        in_specs=[smem()] + [vmem()] * (len(parts) + len(chunks)),
        out_specs=vmem(),
        out_shape=jax.ShapeDtypeStruct((count, rows, columns), jnp.bfloat16),
        cost_estimate=pl.CostEstimate(
            flops=2 * rows * depth * columns * count,
            bytes_accessed=2 * depth * columns * count,
            transcendentals=0,
        ),
        compiler_params=params(),
        name="emit",
    )(start, *parts, *chunks)


def combine_kernel(order_ref, own_ref, other_ref, out_ref):
    width = own_ref.shape[2]
    for k in range(own_ref.shape[0]):
        summed = own_ref[k].astype(jnp.float32) + other_ref[k].astype(jnp.float32)
        start = pl.multiple_of(order_ref[k] * width, width)
        out_ref[:, pl.ds(start, width)] = (residual_scale * summed).astype(jnp.bfloat16)


def combine(own, other, order):
    count, rows, columns = own.shape
    return pl.pallas_call(
        combine_kernel,
        in_specs=[smem(), vmem(), vmem()],
        out_specs=vmem(),
        out_shape=jax.ShapeDtypeStruct((rows, count * columns), jnp.bfloat16),
        compiler_params=params(),
        name="combine",
    )(order, own, other)


def rope_tables(positions, dim):
    half_dim = dim // 2
    frequency = rope_base ** (-(jnp.arange(half_dim, dtype=jnp.float32) * 2.0 / dim))
    angles = positions.astype(jnp.float32)[None, :] * frequency[:, None]
    return jnp.cos(angles), jnp.sin(angles)


def body(req_count, tp_count, tokens, norm_gain, w_query, w_kv, w_out, kv_cache, page_table, cached_len, span_len):
    fast = tp_count == 2 and req_count == 16 and w_out.shape[1] % 128 == 0
    device = lax.axis_index("req")
    rank = lax.axis_index("tp")
    heads = w_kv.shape[1]
    dim = w_kv.shape[2] // 2
    group = w_query.shape[1] // dim // heads
    own_rows = tokens.shape[0]
    weights = jnp.concatenate([w_query, w_kv.reshape(w_kv.shape[0], -1)], axis=1)
    if fast:
        tables = cycle_tables(req_count)
        order = jnp.array(tables[3], jnp.int32)[device]
        blocks, ends = ring_gather(weights, tables)
        other = lax.ppermute(tokens, "tp", [(0, 1), (1, 0)])
        whole = jnp.concatenate(
            [jnp.where(rank == 0, tokens, other), jnp.where(rank == 0, other, tokens)], axis=0
        )
        chunks = blocks + ends
    else:
        order = jnp.zeros((1,), jnp.int32)
        chunks = [lax.all_gather(weights, "req", axis=0, tiled=True)]
        whole = lax.all_gather(tokens, "tp", axis=0, tiled=True)
    hidden = whole.astype(jnp.float32)
    normed = (
        hidden * lax.rsqrt(jnp.mean(hidden * hidden, axis=-1, keepdims=True) + epsilon) * norm_gain
    ).astype(jnp.bfloat16)
    length = lax.dynamic_slice_in_dim(cached_len, device, 1)
    positions = length[0] + jnp.arange(normed.shape[0], dtype=jnp.int32)
    cosine, sines = rope_tables(positions, dim)
    keys, values = prepare(kv_cache, page_table[0], length)
    queries, new_keys, new_values = project(
        normed, chunks, order, cosine, sines, heads, group, dim
    )
    parts = [
        attend(h, keys, values, queries, new_keys, new_values, length, span_len)
        for h in range(heads)
    ]
    if not fast:
        attended = jnp.concatenate(parts, axis=1)
        gathered = lax.all_gather(w_out, "req", axis=1, tiled=True)
        partial = matmul(attended, gathered).astype(jnp.bfloat16)
        summed = lax.psum_scatter(partial, "tp", scatter_dimension=0, tiled=True)
        return (residual_scale * summed.astype(jnp.float32)).astype(jnp.bfloat16)
    blocks, ends = ring_gather(w_out, tables)
    chunks = blocks + ends
    theirs = emit(parts, chunks, ((1 - rank) * own_rows).reshape(1), own_rows, req_count)
    received = lax.ppermute(theirs, "tp", [(0, 1), (1, 0)])
    ours = emit(parts, chunks, (rank * own_rows).reshape(1), own_rows, req_count)
    return combine(ours, received, order)


def solution(mesh):
    in_specs = (
        P(("req", "tp"), None),
        P(),
        P("req", "tp"),
        P("req", "tp", None),
        P("tp", "req"),
        P("req", None, "tp", None),
        P("req", None),
        P(),
        P("req"),
    )
    out_specs = P(("req", "tp"), None)
    program = functools.partial(body, mesh.shape["req"], mesh.shape["tp"])
    return jax.shard_map(
        program, mesh=mesh, in_specs=in_specs, out_specs=out_specs, check_vma=False
    )
```

```python
import functools

import jax
import jax.numpy as jnp
from jax import lax
from jax.experimental import pallas as pl
from jax.experimental.pallas import tpu as pltpu
from jax.sharding import PartitionSpec as P

epsilon = 1e-05
score_scale = 0.015625
residual_scale = 0.22
rope_base = 10000000.0
masked_score = -1e30
key_block = 1024
score_chunk = 256
value_chunk = 256
token_tile = 128


def matmul(a, b):
    return jnp.dot(a, b, preferred_element_type=jnp.float32)


def vmem():
    return pl.BlockSpec(memory_space=pltpu.VMEM)


def smem():
    return pl.BlockSpec(memory_space=pltpu.SMEM)


def params(mebibytes):
    return pltpu.CompilerParams(vmem_limit_bytes=mebibytes * 1024 * 1024)


def cycle_tables(count):
    depth = count // 4
    walk = [(z, 0) for z in range(depth)] + [(z, 1) for z in reversed(range(depth))]
    device = lambda chip, core: (chip[0] * 2 + chip[1]) * 2 + core
    length = len(walk)
    ahead = [
        (device(walk[k], c), device(walk[(k + 1) % length], c))
        for k in range(length)
        for c in range(2)
    ]
    back = [(b, a) for a, b in ahead]
    swap = [(i, i ^ 1) for i in range(count)]
    order = [None] * count
    for k in range(length):
        for c in range(2):
            row = []
            for step in range(length // 2):
                sources = [walk[(k - step) % length], walk[(k + step) % length]]
                for chip in sources[: 1 if step == 0 else 2]:
                    row += [device(chip, c), device(chip, 1 - c)]
            far = walk[(k + length // 2) % length]
            row += [device(far, c), device(far, 1 - c)]
            order[device(walk[k], c)] = row
    return ahead, back, swap, order


def after(value, *others):
    return lax.optimization_barrier((value,) + others)[0]


class Ring:
    def __init__(self, shard, tables):
        self.ahead, self.back, self.swap, self.order = tables
        self.length = len(self.order) // 2
        self.half = shard.shape[0] // 2
        self.up = self.down = shard
        self.blocks = [shard, self.move(shard, self.swap)]

    def move(self, value, pairs):
        return lax.ppermute(value, "req", pairs)

    def step(self, *others):
        if others:
            self.up, self.down = lax.optimization_barrier((self.up, self.down) + others)[:2]
        self.up, self.down = self.move(self.up, self.ahead), self.move(self.down, self.back)
        self.blocks += [
            self.up,
            self.move(self.up, self.swap),
            self.down,
            self.move(self.down, self.swap),
        ]

    def last(self, *others):
        if others:
            self.up, self.down = lax.optimization_barrier((self.up, self.down) + others)[:2]
        first = self.move(self.up[: self.half], self.ahead)
        second = self.move(self.down[self.half :], self.back)
        ends = [first, second, self.move(first, self.swap), self.move(second, self.swap)]
        return self.blocks + ends


def prepare_kernel(heads, page, width, pages_step, first_page, aliased, table_ref, length_ref, *refs):
    pages = refs[:pages_step]
    key_ref, value_ref, wide = refs[pages_step + aliased :]
    step = pl.program_id(0)
    half = width // 2
    rows = value_ref.shape[1]
    pick_row = lax.broadcasted_iota(jnp.int32, (rows, width), 0)
    pick_lane = lax.broadcasted_iota(jnp.int32, (rows, width), 1)
    pick = jnp.where(pick_lane == pick_row + half, 1.0, 0.0).astype(jnp.bfloat16)
    ones = jnp.where(lax.broadcasted_iota(jnp.int32, (rows, page), 0) == half, 1.0, 0.0)
    for i in range(pages_step):
        wide[...] = pages[i][0].astype(jnp.float32)
        first = (first_page + step * pages_step + i) * page
        position = first + lax.broadcasted_iota(jnp.int32, (page, width), 0)
        lane = lax.broadcasted_iota(jnp.int32, (page, width), 1)
        bias = jnp.where((lane == half) & (position >= length_ref[0]), masked_score, 0.0)
        for h in range(heads):
            rows_h = wide[pl.ds(h, page, stride=heads), :]
            key_ref[h, pl.ds(i * page, page), :] = jnp.where(lane < half, rows_h, bias).astype(
                jnp.bfloat16
            )
            turned = lax.dot_general(
                pick,
                rows_h.astype(jnp.bfloat16),
                (((1,), (1,)), ((), ())),
                preferred_element_type=jnp.float32,
            )
            value_ref[h, :, pl.ds(i * page, page)] = (turned + ones).astype(jnp.bfloat16)


def with_ones(turned):
    row = lax.broadcasted_iota(jnp.int32, (16, turned.shape[1]), 0)
    return jnp.concatenate([turned, jnp.where(row == 0, 1.0, 0.0)], axis=0)


def prepare(cache, table, length, part, parts, before):
    pages, page, heads, width = cache.shape
    pages_step = 4
    rows = width // 2 + 16
    total = table.shape[0]
    steps = total // pages_step // parts
    flat = cache.reshape(pages, page * heads, width)
    at = part * steps
    page_spec = lambda i: pl.BlockSpec(
        (1, page * heads, width), lambda j, t, n: (t[(at + j) * pages_step + i], 0, 0)
    )
    kept = [pl.BlockSpec(memory_space=pl.ANY)] * len(before)
    return pl.pallas_call(
        functools.partial(
            prepare_kernel, heads, page, width, pages_step, at * pages_step, len(before)
        ),
        grid_spec=pltpu.PrefetchScalarGridSpec(
            num_scalar_prefetch=2,
            grid=(steps,),
            in_specs=[page_spec(i) for i in range(pages_step)] + kept,
            out_specs=[
                pl.BlockSpec((heads, pages_step * page, width), lambda j, t, n: (0, at + j, 0)),
                pl.BlockSpec((heads, rows, pages_step * page), lambda j, t, n: (0, 0, at + j)),
            ],
            scratch_shapes=[pltpu.VMEM((page * heads, width), jnp.float32)],
        ),
        out_shape=[
            jax.ShapeDtypeStruct((heads, total * page, width), jnp.bfloat16),
            jax.ShapeDtypeStruct((heads, rows, total * page), jnp.bfloat16),
        ],
        input_output_aliases={2 + pages_step + i: i for i in range(len(before))},
        cost_estimate=pl.CostEstimate(
            flops=0,
            bytes_accessed=3 * cache.size * cache.dtype.itemsize // parts,
            transcendentals=0,
        ),
        compiler_params=params(16),
        name="prepare",
    )(table, length, *([flat] * pages_step), *before)


def turn(pair, cosine, sines):
    half = pair.shape[0] // 2
    first, second = pair[:half], pair[half:]
    return jnp.concatenate(
        [first * cosine - second * sines, second * cosine + first * sines], axis=0
    )


def assembled(chunks, order_ref, weight):
    if len(chunks) == 1:
        return chunks[0]
    count = order_ref.shape[0]
    rows = weight.shape[0] // count
    for k in range(count):
        start = pl.multiple_of(order_ref[k] * rows, rows)
        if k < count - 2:
            weight[pl.ds(start, rows), :] = chunks[k][...]
        else:
            at = 2 * k - (count - 2)
            weight[pl.ds(start, rows), :] = jnp.concatenate(
                [chunks[at][...], chunks[at + 1][...]], axis=0
            )
    return weight


def query_kernel(heads, group, dim, blocks, order_ref, *refs):
    normed_ref, cos_ref, sin_ref, query_ref, weight = refs[blocks:]
    source = assembled(refs[:blocks], order_ref, weight)
    cosine, sines = cos_ref[...], sin_ref[...]
    tokens = cosine.shape[1]
    normed = normed_ref[...]
    width = group * dim
    row = lax.broadcasted_iota(jnp.int32, (dim, group * token_tile), 0)
    one_row = jnp.where(row == 0, 1.0, 0.0).astype(jnp.bfloat16)
    for h in range(heads):
        turned = jnp.transpose(matmul(normed, source[:, pl.ds(h * width, width)]))
        for g in range(group):
            rotated = turn(turned[g * dim : (g + 1) * dim], cosine, sines).astype(jnp.bfloat16)
            scaled = (rotated.astype(jnp.float32) * score_scale).astype(jnp.bfloat16)
            for q in range(tokens // token_tile):
                query_ref[h, q, pl.ds(0, dim), pl.ds(g * token_tile, token_tile)] = scaled[
                    :, q * token_tile : (q + 1) * token_tile
                ]
        for q in range(tokens // token_tile):
            query_ref[h, q, pl.ds(dim, dim), :] = one_row


def new_kernel(heads, dim, blocks, order_ref, *refs):
    normed_ref, cos_ref, sin_ref, key_ref, value_ref, weight = refs[blocks:]
    source = assembled(refs[:blocks], order_ref, weight)
    cosine, sines = cos_ref[...], sin_ref[...]
    normed = normed_ref[...]
    for h in range(heads):
        turned = jnp.transpose(matmul(normed, source[:, pl.ds(h * 2 * dim, 2 * dim)]))
        keys = turn(turned[:dim], cosine, sines)
        padded = jnp.concatenate([keys, jnp.zeros_like(keys)], axis=0)
        key_ref[h] = jnp.transpose(padded).astype(jnp.bfloat16)
        value_ref[h] = with_ones(turned[dim:]).astype(jnp.bfloat16)


def project(kernel, name, outs, normed, chunks, order, cosine, sines):
    tokens, width = normed.shape
    columns = chunks[0].shape[1]
    return pl.pallas_call(
        kernel,
        in_specs=[smem()] + [vmem()] * (len(chunks) + 3),
        out_specs=[vmem()] * len(outs),
        out_shape=[jax.ShapeDtypeStruct(shape, jnp.bfloat16) for shape in outs],
        scratch_shapes=[pltpu.VMEM((width, columns), jnp.bfloat16)],
        cost_estimate=pl.CostEstimate(
            flops=2 * tokens * width * columns,
            bytes_accessed=2 * width * columns,
            transcendentals=0,
        ),
        compiler_params=params(24),
        name=name,
    )(order, *chunks, normed, cosine, sines)


def project_query(normed, chunks, order, cosine, sines, heads, group, dim):
    tokens = normed.shape[0]
    outs = [(heads, tokens // token_tile, 2 * dim, group * token_tile)]
    kernel = functools.partial(query_kernel, heads, group, dim, len(chunks))
    return project(kernel, "query", outs, normed, chunks, order, cosine, sines)[0]


def project_new(normed, chunks, order, cosine, sines, heads, dim):
    tokens = normed.shape[0]
    outs = [(heads, tokens, 2 * dim), (heads, dim + 16, tokens)]
    kernel = functools.partial(new_kernel, heads, dim, len(chunks))
    return project(kernel, "new", outs, normed, chunks, order, cosine, sines)


def attend_kernel(
    group,
    dim,
    length_ref,
    span_ref,
    tile_ref,
    key_ref,
    value_ref,
    query_ref,
    new_key_ref,
    new_value_ref,
    out_ref,
    even,
    odd,
):
    lanes = query_ref.shape[3]
    span = new_key_ref.shape[1]
    length = length_ref[0]
    valid = span_ref[0]
    pair = 2 * key_block
    pairs = (length + pair - 1) // pair
    last_block = jnp.maximum(2 * pairs - 1, 0)

    def column_max(scores):
        return jnp.max(scores.reshape(scores.shape[0] // 8, 8, lanes), axis=0)

    q = tile_ref[0]

    def tile():
        def scores_of(block, c, target):
            start = pl.multiple_of(block * key_block + c * score_chunk, score_chunk)
            scores = matmul(key_ref[0, pl.ds(start, score_chunk), :], query_ref[0, q])
            target[pl.ds(c * score_chunk, score_chunk), :] = scores
            return column_max(scores)

        scores = matmul(new_key_ref[0], query_ref[0, q])
        source = lax.broadcasted_iota(jnp.int32, (span, lanes), 0)
        lane = lax.broadcasted_iota(jnp.int32, (span, lanes), 1)
        token = q * token_tile + lax.rem(lane, token_tile)
        scores = jnp.where((source <= token) & (source < valid), scores, masked_score)
        maximum = jnp.max(column_max(scores), axis=0, keepdims=True)
        weights = jnp.exp(scores - maximum).astype(jnp.bfloat16)
        total = matmul(new_value_ref[0], weights)

        top = scores_of(0, 0, even)
        for c in range(1, key_block // score_chunk):
            top = jnp.maximum(top, scores_of(0, c, even))

        def half(block, following, current, target, state):
            maximum, top, total = state
            new_maximum = jnp.maximum(maximum, jnp.max(top, axis=0, keepdims=True))
            total = total * jnp.exp(maximum - new_maximum)
            next_top = None
            ratio = value_chunk // score_chunk
            parts = []
            for c in range(key_block // score_chunk):
                seen = scores_of(following, c, target)
                next_top = seen if next_top is None else jnp.maximum(next_top, seen)
                part = jnp.exp(current[pl.ds(c * score_chunk, score_chunk), :] - new_maximum)
                parts.append(part.astype(jnp.bfloat16))
                if len(parts) == ratio:
                    weights = parts[0] if ratio == 1 else jnp.concatenate(parts, axis=0)
                    start = block * key_block + (c + 1 - ratio) * score_chunk
                    start = pl.multiple_of(start, value_chunk)
                    total = total + matmul(value_ref[0, :, pl.ds(start, value_chunk)], weights)
                    parts = []
            return new_maximum, next_top, total

        def advance(i, state):
            block = 2 * i
            state = half(block, block + 1, even, odd, state)
            following = jnp.minimum(block + 2, last_block)
            return half(block + 1, following, odd, even, state)

        _, _, total = lax.fori_loop(0, pairs, advance, (maximum, top, total))
        result = total[:dim] / total[dim : dim + 1]
        row = q * token_tile + lax.broadcasted_iota(jnp.int32, (token_tile, 2 * dim), 0)
        for g in range(0, group, 2):
            both = jnp.concatenate(
                [
                    result[:, g * token_tile : (g + 1) * token_tile],
                    result[:, (g + 1) * token_tile : (g + 2) * token_tile],
                ],
                axis=0,
            )
            kept = jnp.where(row < valid, jnp.transpose(both), 0.0)
            out_ref[:, pl.ds(g * dim, 2 * dim)] = kept.astype(jnp.bfloat16)

    pl.when(q * token_tile < valid)(tile)

    @pl.when(q * token_tile >= valid)
    def empty():
        out_ref[...] = jnp.zeros_like(out_ref)


def attend(head, tile, keys, values, queries, new_keys, new_values, length, valid):
    _, cached, width = keys.shape
    dim = width // 2
    lanes = queries.shape[3]
    group = lanes // token_tile
    block = lambda array: pl.BlockSpec(
        (1,) + array.shape[1:], lambda i: (head,) + (0,) * (array.ndim - 1)
    )
    arrays = (keys, values, queries, new_keys, new_values)
    return pl.pallas_call(
        functools.partial(attend_kernel, group, dim),
        grid=(1,),
        in_specs=[smem()] * 3 + [block(a) for a in arrays],
        out_specs=pl.BlockSpec((token_tile, group * dim), lambda i: (0, 0)),
        out_shape=jax.ShapeDtypeStruct((token_tile, group * dim), jnp.bfloat16),
        scratch_shapes=[pltpu.VMEM((key_block, lanes), jnp.float32)] * 2,
        cost_estimate=pl.CostEstimate(
            flops=2 * cached * lanes * 2 * width,
            bytes_accessed=2 * cached * 2 * width,
            transcendentals=cached * lanes,
        ),
        compiler_params=params(24),
        name="attend",
    )(length, valid, tile, *arrays)


def emit_kernel(heads, blocks, *refs):
    parts = refs[:heads]
    chunks = refs[heads : heads + blocks]
    out_ref = refs[heads + blocks]
    attended = jnp.concatenate([p[...] for p in parts], axis=1)
    count = out_ref.shape[0]
    for k in range(0, count, 2):
        if k < count - 2:
            weight = jnp.concatenate([chunks[k][...], chunks[k + 1][...]], axis=1)
        else:
            at = count - 2
            own = jnp.concatenate([chunks[at][...], chunks[at + 1][...]], axis=0)
            other = jnp.concatenate([chunks[at + 2][...], chunks[at + 3][...]], axis=0)
            weight = jnp.concatenate([own, other], axis=1)
        both = matmul(attended, weight).astype(jnp.bfloat16)
        width = both.shape[1] // 2
        out_ref[k] = both[:, :width]
        out_ref[k + 1] = both[:, width:]


def emit(parts, chunks, count):
    columns = chunks[0].shape[1]
    depth = chunks[0].shape[0]
    rows = parts[0].shape[0]
    return pl.pallas_call(
        functools.partial(emit_kernel, len(parts), len(chunks)),
        in_specs=[vmem()] * (len(parts) + len(chunks)),
        out_specs=vmem(),
        out_shape=jax.ShapeDtypeStruct((count, rows, columns), jnp.bfloat16),
        cost_estimate=pl.CostEstimate(
            flops=2 * rows * depth * columns * count,
            bytes_accessed=2 * depth * columns * count,
            transcendentals=0,
        ),
        compiler_params=params(24),
        name="emit",
    )(*parts, *chunks)


def combine_kernel(order_ref, own_ref, other_ref, out_ref):
    width = own_ref.shape[2]
    for k in range(own_ref.shape[0]):
        summed = own_ref[k].astype(jnp.float32) + other_ref[k].astype(jnp.float32)
        start = pl.multiple_of(order_ref[k] * width, width)
        out_ref[:, pl.ds(start, width)] = (residual_scale * summed).astype(jnp.bfloat16)


def combine(own, other, order):
    count, rows, columns = own.shape
    return pl.pallas_call(
        combine_kernel,
        in_specs=[smem(), vmem(), vmem()],
        out_specs=vmem(),
        out_shape=jax.ShapeDtypeStruct((rows, count * columns), jnp.bfloat16),
        compiler_params=params(16),
        name="combine",
    )(order, own, other)


def rope_tables(positions, dim):
    half_dim = dim // 2
    frequency = rope_base ** (-(jnp.arange(half_dim, dtype=jnp.float32) * 2.0 / dim))
    angles = positions.astype(jnp.float32)[None, :] * frequency[:, None]
    return jnp.cos(angles), jnp.sin(angles)


def body(req_count, tp_count, tokens, norm_gain, w_query, w_kv, w_out, kv_cache, page_table, cached_len, span_len):
    fast = tp_count == 2 and req_count == 16 and w_out.shape[1] % 128 == 0 and w_kv.shape[1] == 4
    device = lax.axis_index("req")
    rank = lax.axis_index("tp")
    heads = w_kv.shape[1]
    dim = w_kv.shape[2] // 2
    group = w_query.shape[1] // dim // heads
    own_rows = tokens.shape[0]
    length = lax.dynamic_slice_in_dim(cached_len, device, 1)
    table = page_table[0]
    if fast:
        tables = cycle_tables(req_count)
        order = jnp.array(tables[3], jnp.int32)[device]
        swap = [(0, 1), (1, 0)]
        ring_query = Ring(w_query, tables)
        ring_new = Ring(w_kv.reshape(w_kv.shape[0], -1), tables)
        ring_out = Ring(w_out, tables)
        other = lax.ppermute(tokens, "tp", swap)
        whole = jnp.concatenate(
            [jnp.where(rank == 0, tokens, other), jnp.where(rank == 0, other, tokens)], axis=0
        )
        parts = 4
        state = ()
        for part in range(parts):
            if part < parts - 1:
                ring_query.step(*state[:1])
                ring_new.step(*state[:1])
            else:
                query_chunks = ring_query.last(*state[:1])
                new_chunks = ring_new.last(*state[:1])
            state = prepare(kv_cache, table, length, part, parts, state)
        keys, values = state
    else:
        order = jnp.zeros((1,), jnp.int32)
        gather = lambda array: lax.all_gather(array, "req", axis=0, tiled=True)
        query_chunks = [gather(w_query)]
        new_chunks = [gather(w_kv.reshape(w_kv.shape[0], -1))]
        whole = lax.all_gather(tokens, "tp", axis=0, tiled=True)
        keys, values = prepare(kv_cache, table, length, 0, 1, ())
    hidden = whole.astype(jnp.float32)
    normed = (
        hidden * lax.rsqrt(jnp.mean(hidden * hidden, axis=-1, keepdims=True) + epsilon) * norm_gain
    ).astype(jnp.bfloat16)
    positions = length[0] + jnp.arange(normed.shape[0], dtype=jnp.int32)
    cosine, sines = rope_tables(positions, dim)
    new_keys, new_values = project_new(normed, new_chunks, order, cosine, sines, heads, dim)
    queries = project_query(normed, query_chunks, order, cosine, sines, heads, group, dim)

    def attend_at(head, tile, valid):
        return attend(head, tile, keys, values, queries, new_keys, new_values, length, valid)

    if not fast:
        tiles = [jnp.full((1,), q, jnp.int32) for q in range(normed.shape[0] // token_tile)]
        attended = jnp.concatenate(
            [
                jnp.concatenate([attend_at(h, tile, span_len) for h in range(heads)], axis=1)
                for tile in tiles
            ],
            axis=0,
        )
        gathered = lax.all_gather(w_out, "req", axis=1, tiled=True)
        partial = matmul(attended, gathered).astype(jnp.bfloat16)
        summed = lax.psum_scatter(partial, "tp", scatter_dimension=0, tiled=True)
        return (residual_scale * summed.astype(jnp.float32)).astype(jnp.bfloat16)
    theirs, ours = (1 - rank).reshape(1), rank.reshape(1)
    ring_out.step(ring_query.up)
    ring_out.step(queries)
    first = [attend_at(0, theirs, span_len)]
    first.append(attend_at(1, theirs, after(span_len, first[-1])))
    ring_out.step(first[-1])
    first.append(attend_at(2, theirs, after(span_len, first[-1])))
    first.append(attend_at(3, theirs, after(span_len, first[-1])))
    out_chunks = ring_out.last(first[-1])
    second = [attend_at(0, ours, after(span_len, first[-1]))]
    second.append(attend_at(1, ours, after(span_len, second[-1])))
    sent = emit(first, [after(out_chunks[0], second[-1])] + out_chunks[1:], req_count)
    received = lax.ppermute(sent, "tp", swap)
    second.append(attend_at(2, ours, after(span_len, sent)))
    second.append(attend_at(3, ours, after(span_len, second[-1])))
    kept = emit(second, out_chunks, req_count)
    return combine(kept, received, order)


def solution(mesh):
    in_specs = (
        P(("req", "tp"), None),
        P(),
        P("req", "tp"),
        P("req", "tp", None),
        P("tp", "req"),
        P("req", None, "tp", None),
        P("req", None),
        P(),
        P("req"),
    )
    out_specs = P(("req", "tp"), None)
    program = functools.partial(body, mesh.shape["req"], mesh.shape["tp"])
    return jax.shard_map(
        program, mesh=mesh, in_specs=in_specs, out_specs=out_specs, check_vma=False
    )
```

```python
import functools

import jax
import jax.numpy as jnp
from jax import lax
from jax.experimental import pallas as pl
from jax.experimental.pallas import tpu as pltpu
from jax.sharding import PartitionSpec as P

epsilon = 1e-05
score_scale = 0.015625
residual_scale = 0.22
rope_base = 10000000.0
masked_score = -1e30
key_block = 1024
score_chunk = 256
value_chunk = 256
token_tile = 128


def matmul(a, b):
    return jnp.dot(a, b, preferred_element_type=jnp.float32)


def vmem():
    return pl.BlockSpec(memory_space=pltpu.VMEM)


def smem():
    return pl.BlockSpec(memory_space=pltpu.SMEM)


def params(mebibytes):
    return pltpu.CompilerParams(vmem_limit_bytes=mebibytes * 1024 * 1024)


def cycle_tables(count):
    depth = count // 4
    walk = [(z, 0) for z in range(depth)] + [(z, 1) for z in reversed(range(depth))]
    device = lambda chip, core: (chip[0] * 2 + chip[1]) * 2 + core
    length = len(walk)
    ahead = [
        (device(walk[k], c), device(walk[(k + 1) % length], c))
        for k in range(length)
        for c in range(2)
    ]
    back = [(b, a) for a, b in ahead]
    swap = [(i, i ^ 1) for i in range(count)]
    order = [None] * count
    for k in range(length):
        for c in range(2):
            row = []
            for step in range(length // 2):
                sources = [walk[(k - step) % length], walk[(k + step) % length]]
                for chip in sources[: 1 if step == 0 else 2]:
                    row += [device(chip, c), device(chip, 1 - c)]
            far = walk[(k + length // 2) % length]
            row += [device(far, c), device(far, 1 - c)]
            order[device(walk[k], c)] = row
    return ahead, back, swap, order


def after(value, *others):
    return lax.optimization_barrier((value,) + others)[0]


class Ring:
    def __init__(self, shard, tables):
        self.ahead, self.back, self.swap, self.order = tables
        self.length = len(self.order) // 2
        self.half = shard.shape[0] // 2
        self.up = self.down = shard
        self.blocks = [shard, self.move(shard, self.swap)]

    def move(self, value, pairs):
        return lax.ppermute(value, "req", pairs)

    def step(self, *others):
        if others:
            self.up, self.down = lax.optimization_barrier((self.up, self.down) + others)[:2]
        self.up, self.down = self.move(self.up, self.ahead), self.move(self.down, self.back)
        self.blocks += [
            self.up,
            self.move(self.up, self.swap),
            self.down,
            self.move(self.down, self.swap),
        ]

    def last(self, *others):
        if others:
            self.up, self.down = lax.optimization_barrier((self.up, self.down) + others)[:2]
        first = self.move(self.up[: self.half], self.ahead)
        second = self.move(self.down[self.half :], self.back)
        ends = [first, second, self.move(first, self.swap), self.move(second, self.swap)]
        return self.blocks + ends


def prepare_kernel(heads, page, width, pages_step, first_page, aliased, table_ref, length_ref, *refs):
    pages = refs[:pages_step]
    key_ref, value_ref, wide = refs[pages_step + aliased :]
    step = pl.program_id(0)
    half = width // 2
    rows = value_ref.shape[1]
    pick_row = lax.broadcasted_iota(jnp.int32, (rows, width), 0)
    pick_lane = lax.broadcasted_iota(jnp.int32, (rows, width), 1)
    pick = jnp.where(pick_lane == pick_row + half, 1.0, 0.0).astype(jnp.bfloat16)
    ones = jnp.where(lax.broadcasted_iota(jnp.int32, (rows, page), 0) == half, 1.0, 0.0)
    for i in range(pages_step):
        wide[...] = pages[i][0].astype(jnp.float32)
        first = (first_page + step * pages_step + i) * page
        position = first + lax.broadcasted_iota(jnp.int32, (page, width), 0)
        lane = lax.broadcasted_iota(jnp.int32, (page, width), 1)
        bias = jnp.where((lane == half) & (position >= length_ref[0]), masked_score, 0.0)
        for h in range(heads):
            rows_h = wide[pl.ds(h, page, stride=heads), :]
            key_ref[h, pl.ds(i * page, page), :] = jnp.where(lane < half, rows_h, bias).astype(
                jnp.bfloat16
            )
            turned = lax.dot_general(
                pick,
                rows_h.astype(jnp.bfloat16),
                (((1,), (1,)), ((), ())),
                preferred_element_type=jnp.float32,
            )
            value_ref[h, :, pl.ds(i * page, page)] = (turned + ones).astype(jnp.bfloat16)


def with_ones(turned):
    row = lax.broadcasted_iota(jnp.int32, (16, turned.shape[1]), 0)
    return jnp.concatenate([turned, jnp.where(row == 0, 1.0, 0.0)], axis=0)


def prepare(cache, table, length, part, parts, before):
    pages, page, heads, width = cache.shape
    pages_step = 4
    rows = width // 2 + 16
    total = table.shape[0]
    steps = total // pages_step // parts
    flat = cache.reshape(pages, page * heads, width)
    at = part * steps
    page_spec = lambda i: pl.BlockSpec(
        (1, page * heads, width), lambda j, t, n: (t[(at + j) * pages_step + i], 0, 0)
    )
    kept = [pl.BlockSpec(memory_space=pl.ANY)] * len(before)
    return pl.pallas_call(
        functools.partial(
            prepare_kernel, heads, page, width, pages_step, at * pages_step, len(before)
        ),
        grid_spec=pltpu.PrefetchScalarGridSpec(
            num_scalar_prefetch=2,
            grid=(steps,),
            in_specs=[page_spec(i) for i in range(pages_step)] + kept,
            out_specs=[
                pl.BlockSpec((heads, pages_step * page, width), lambda j, t, n: (0, at + j, 0)),
                pl.BlockSpec((heads, rows, pages_step * page), lambda j, t, n: (0, 0, at + j)),
            ],
            scratch_shapes=[pltpu.VMEM((page * heads, width), jnp.float32)],
        ),
        out_shape=[
            jax.ShapeDtypeStruct((heads, total * page, width), jnp.bfloat16),
            jax.ShapeDtypeStruct((heads, rows, total * page), jnp.bfloat16),
        ],
        input_output_aliases={2 + pages_step + i: i for i in range(len(before))},
        cost_estimate=pl.CostEstimate(
            flops=0,
            bytes_accessed=3 * cache.size * cache.dtype.itemsize // parts,
            transcendentals=0,
        ),
        compiler_params=params(60),
        name="prepare",
    )(table, length, *([flat] * pages_step), *before)


def turn(pair, cosine, sines):
    half = pair.shape[0] // 2
    first, second = pair[:half], pair[half:]
    return jnp.concatenate(
        [first * cosine - second * sines, second * cosine + first * sines], axis=0
    )


def assembled(chunks, order_ref, weight):
    if len(chunks) == 1:
        return chunks[0]
    count = order_ref.shape[0]
    rows = weight.shape[0] // count
    for k in range(count):
        start = pl.multiple_of(order_ref[k] * rows, rows)
        if k < count - 2:
            weight[pl.ds(start, rows), :] = chunks[k][...]
        else:
            at = 2 * k - (count - 2)
            weight[pl.ds(start, rows), :] = jnp.concatenate(
                [chunks[at][...], chunks[at + 1][...]], axis=0
            )
    return weight


def project_kernel(heads, new_heads, group, dim, blocks, order_ref, *refs):
    normed_ref, cos_ref, sin_ref = refs[blocks : blocks + 3]
    query_ref = refs[blocks + 3]
    source = assembled(refs[:blocks], order_ref, refs[-1])
    cosine, sines = cos_ref[...], sin_ref[...]
    tokens = cosine.shape[1]
    normed = normed_ref[...]
    width = group * dim
    row = lax.broadcasted_iota(jnp.int32, (dim, group * token_tile), 0)
    one_row = jnp.where(row == 0, 1.0, 0.0).astype(jnp.bfloat16)
    for h in range(heads):
        turned = jnp.transpose(matmul(normed, source[:, pl.ds(h * width, width)]))
        for g in range(group):
            rotated = turn(turned[g * dim : (g + 1) * dim], cosine, sines).astype(jnp.bfloat16)
            scaled = (rotated.astype(jnp.float32) * score_scale).astype(jnp.bfloat16)
            for q in range(tokens // token_tile):
                query_ref[h, q, pl.ds(0, dim), pl.ds(g * token_tile, token_tile)] = scaled[
                    :, q * token_tile : (q + 1) * token_tile
                ]
        for q in range(tokens // token_tile):
            query_ref[h, q, pl.ds(dim, dim), :] = one_row
    for h in range(new_heads):
        key_ref, value_ref = refs[blocks + 4 : blocks + 6]
        at = heads * width + h * 2 * dim
        turned = jnp.transpose(matmul(normed, source[:, pl.ds(at, 2 * dim)]))
        keys = turn(turned[:dim], cosine, sines)
        padded = jnp.concatenate([keys, jnp.zeros_like(keys)], axis=0)
        key_ref[h] = jnp.transpose(padded).astype(jnp.bfloat16)
        value_ref[h] = with_ones(turned[dim:]).astype(jnp.bfloat16)


def project(normed, chunks, order, cosine, sines, heads, new_heads, group, dim):
    tokens, width = normed.shape
    columns = chunks[0].shape[1]
    outs = [(heads, tokens // token_tile, 2 * dim, group * token_tile)]
    if new_heads:
        outs += [(new_heads, tokens, 2 * dim), (new_heads, dim + 16, tokens)]
    return pl.pallas_call(
        functools.partial(project_kernel, heads, new_heads, group, dim, len(chunks)),
        in_specs=[smem()] + [vmem()] * (len(chunks) + 3),
        out_specs=[vmem()] * len(outs),
        out_shape=[jax.ShapeDtypeStruct(shape, jnp.bfloat16) for shape in outs],
        scratch_shapes=[pltpu.VMEM((width, columns), jnp.bfloat16)],
        cost_estimate=pl.CostEstimate(
            flops=2 * tokens * width * columns,
            bytes_accessed=2 * width * columns,
            transcendentals=0,
        ),
        compiler_params=params(24),
        name="project",
    )(order, *chunks, normed, cosine, sines)


def column_max(scores):
    return jnp.max(scores.reshape(scores.shape[0] // 8, 8, scores.shape[1]), axis=0)


def attend_kernel(
    head,
    cache_head,
    length_ref,
    span_ref,
    tile_ref,
    keys_hbm,
    values_hbm,
    query_ref,
    out_ref,
    token_ref,
    even,
    odd,
    key_ref,
    value_ref,
    key_sems,
    value_sems,
):
    lanes = query_ref.shape[3]
    length = length_ref[0]
    token_ref[0] = length
    q = tile_ref[0]
    pair = 2 * key_block
    sum_row = values_hbm.shape[1] - 16
    live = q * token_tile < span_ref[0]
    pairs = jnp.where(live, (length + pair - 1) // pair, 0)
    last_block = jnp.maximum(2 * pairs - 1, 0)

    def key_copy(i):
        piece = pl.ds(pl.multiple_of(i * pair, pair), pair)
        return pltpu.make_async_copy(
            keys_hbm.at[cache_head, piece], key_ref.at[piece], key_sems.at[i]
        )

    def value_copy(i):
        piece = pl.ds(pl.multiple_of(i * pair, pair), pair)
        return pltpu.make_async_copy(
            values_hbm.at[cache_head, :, piece], value_ref.at[:, piece], value_sems.at[i]
        )

    for i in range(keys_hbm.shape[1] // pair):

        @pl.when(i < pairs)
        def fetch():
            key_copy(i).start()
            value_copy(i).start()

    def scores_of(block, c, target):
        start = pl.multiple_of(block * key_block + c * score_chunk, score_chunk)
        scores = matmul(key_ref[pl.ds(start, score_chunk), :], query_ref[head, q])
        target[pl.ds(c * score_chunk, score_chunk), :] = scores
        return column_max(scores)

    def half(block, following, current, target, state):
        maximum, top, total = state
        new_maximum = jnp.maximum(maximum, jnp.max(top, axis=0, keepdims=True))
        total = total * jnp.exp(maximum - new_maximum)
        next_top = None
        ratio = value_chunk // score_chunk
        parts = []
        for c in range(key_block // score_chunk):
            seen = scores_of(following, c, target)
            next_top = seen if next_top is None else jnp.maximum(next_top, seen)
            part = jnp.exp(current[pl.ds(c * score_chunk, score_chunk), :] - new_maximum)
            parts.append(part.astype(jnp.bfloat16))
            if len(parts) == ratio:
                weights = parts[0] if ratio == 1 else jnp.concatenate(parts, axis=0)
                start = block * key_block + (c + 1 - ratio) * score_chunk
                start = pl.multiple_of(start, value_chunk)
                total = total + matmul(value_ref[:, pl.ds(start, value_chunk)], weights)
                parts = []
        return new_maximum, next_top, total

    def advance(i, state):
        @pl.when(i + 1 < pairs)
        def arrived():
            key_copy(i + 1).wait()

        value_copy(i).wait()
        block = 2 * i
        state = half(block, block + 1, even, odd, state)
        following = jnp.minimum(block + 2, last_block)
        return half(block + 1, following, odd, even, state)

    @pl.when(pairs > 0)
    def work():
        key_copy(0).wait()
        top = scores_of(0, 0, even)
        for c in range(1, key_block // score_chunk):
            top = jnp.maximum(top, scores_of(0, c, even))
        start = (
            jnp.full((1, lanes), masked_score, jnp.float32),
            top,
            jnp.zeros(out_ref.shape, jnp.float32),
        )
        maximum, _, total = lax.fori_loop(0, pairs, advance, start)
        row = lax.broadcasted_iota(jnp.int32, out_ref.shape, 0)
        out_ref[...] = jnp.where(row == sum_row + 1, maximum, total)

    @pl.when(pairs == 0)
    def nothing():
        row = lax.broadcasted_iota(jnp.int32, out_ref.shape, 0)
        out_ref[...] = jnp.where(row == sum_row + 1, masked_score, 0.0)


def attend(head, cache_head, tile, keys, values, queries, token, valid):
    _, cached, width = keys.shape
    rows = values.shape[1]
    lanes = queries.shape[3]
    pieces = cached // (2 * key_block)
    anywhere = pl.BlockSpec(memory_space=pl.ANY)
    return pl.pallas_call(
        functools.partial(attend_kernel, head, cache_head),
        in_specs=[smem()] * 3 + [anywhere, anywhere, vmem()],
        out_specs=[vmem(), smem()],
        out_shape=[
            jax.ShapeDtypeStruct((rows, lanes), jnp.float32),
            jax.ShapeDtypeStruct((1,), jnp.int32),
        ],
        scratch_shapes=[pltpu.VMEM((key_block, lanes), jnp.float32)] * 2
        + [
            pltpu.VMEM((cached, width), jnp.bfloat16),
            pltpu.VMEM((rows, cached), jnp.bfloat16),
            pltpu.SemaphoreType.DMA((pieces,)),
            pltpu.SemaphoreType.DMA((pieces,)),
        ],
        cost_estimate=pl.CostEstimate(
            flops=2 * cached * lanes * 2 * width,
            bytes_accessed=2 * cached * 2 * width,
            transcendentals=cached * lanes,
        ),
        compiler_params=params(60),
        name="attend",
    )(token, valid, tile, keys, values, queries)


def finish_head(q, valid, group, dim, state, query, new_key, new_value):
    lanes = query.shape[1]
    span = new_key.shape[0]
    scores = matmul(new_key, query)
    source = lax.broadcasted_iota(jnp.int32, (span, lanes), 0)
    lane = lax.broadcasted_iota(jnp.int32, (span, lanes), 1)
    position = q * token_tile + lax.rem(lane, token_tile)
    scores = jnp.where((source <= position) & (source < valid), scores, masked_score)
    cached_maximum = state[dim + 1 : dim + 2]
    maximum = jnp.maximum(jnp.max(column_max(scores), axis=0, keepdims=True), cached_maximum)
    weights = jnp.exp(scores - maximum).astype(jnp.bfloat16)
    total = state * jnp.exp(cached_maximum - maximum) + matmul(new_value, weights)
    result = total[:dim] / total[dim : dim + 1]
    row = q * token_tile + lax.broadcasted_iota(jnp.int32, (token_tile, 2 * dim), 0)
    pieces = []
    for g in range(0, group, 2):
        both = jnp.concatenate(
            [
                result[:, g * token_tile : (g + 1) * token_tile],
                result[:, (g + 1) * token_tile : (g + 2) * token_tile],
            ],
            axis=0,
        )
        pieces.append(jnp.where(row < valid, jnp.transpose(both), 0.0).astype(jnp.bfloat16))
    return pieces


def finish_kernel(heads, group, dim, sets, blocks, span_ref, tile_ref, *refs):
    states = refs[:heads]
    queries = refs[heads : heads + sets]
    new_key_ref, new_value_ref = refs[heads + sets : heads + sets + 2]
    chunks = refs[heads + sets + 2 : heads + sets + 2 + blocks]
    out_ref = refs[heads + sets + 2 + blocks]
    q = tile_ref[0]
    pieces = []
    for h in range(heads):
        per_set = heads // sets
        query = queries[h // per_set][h % per_set, q]
        pieces += finish_head(
            q, span_ref[0], group, dim, states[h][...], query, new_key_ref[h], new_value_ref[h]
        )
    attended = jnp.concatenate(pieces, axis=1)
    if blocks == 0:
        out_ref[...] = attended
        return
    token_ref = refs[heads + sets + 3 + blocks]
    token_ref[0] = q
    count = out_ref.shape[0]
    for k in range(0, count, 2):
        if k < count - 2:
            weight = jnp.concatenate([chunks[k][...], chunks[k + 1][...]], axis=1)
        else:
            at = count - 2
            own = jnp.concatenate([chunks[at][...], chunks[at + 1][...]], axis=0)
            other = jnp.concatenate([chunks[at + 2][...], chunks[at + 3][...]], axis=0)
            weight = jnp.concatenate([own, other], axis=1)
        both = matmul(attended, weight).astype(jnp.bfloat16)
        width = both.shape[1] // 2
        out_ref[k] = both[:, :width]
        out_ref[k + 1] = both[:, width:]


def finish(states, tile, valid, queries, new_keys, new_values, group, chunks, count):
    heads = len(states)
    dim = states[0].shape[0] - 16
    if chunks:
        columns = chunks[0].shape[1]
        out_shape = [
            jax.ShapeDtypeStruct((count, token_tile, columns), jnp.bfloat16),
            jax.ShapeDtypeStruct((1,), jnp.int32),
        ]
        out_specs = [vmem(), smem()]
    else:
        columns = 0
        out_shape = [jax.ShapeDtypeStruct((token_tile, heads * group * dim), jnp.bfloat16)]
        out_specs = [vmem()]
    depth = heads * group * dim
    return pl.pallas_call(
        functools.partial(finish_kernel, heads, group, dim, len(queries), len(chunks)),
        in_specs=[smem()] * 2 + [vmem()] * (heads + len(queries) + 2 + len(chunks)),
        out_specs=out_specs,
        out_shape=out_shape,
        cost_estimate=pl.CostEstimate(
            flops=2 * token_tile * depth * columns * count,
            bytes_accessed=2 * depth * columns * count,
            transcendentals=0,
        ),
        compiler_params=params(24),
        name="finish",
    )(valid, tile, *states, *queries, new_keys, new_values, *chunks)


def combine_kernel(order_ref, own_ref, other_ref, out_ref):
    width = own_ref.shape[2]
    for k in range(own_ref.shape[0]):
        summed = own_ref[k].astype(jnp.float32) + other_ref[k].astype(jnp.float32)
        start = pl.multiple_of(order_ref[k] * width, width)
        out_ref[:, pl.ds(start, width)] = (residual_scale * summed).astype(jnp.bfloat16)


def combine(own, other, order):
    count, rows, columns = own.shape
    return pl.pallas_call(
        combine_kernel,
        in_specs=[smem(), vmem(), vmem()],
        out_specs=vmem(),
        out_shape=jax.ShapeDtypeStruct((rows, count * columns), jnp.bfloat16),
        compiler_params=params(16),
        name="combine",
    )(order, own, other)


def rope_tables(positions, dim):
    half_dim = dim // 2
    frequency = rope_base ** (-(jnp.arange(half_dim, dtype=jnp.float32) * 2.0 / dim))
    angles = positions.astype(jnp.float32)[None, :] * frequency[:, None]
    return jnp.cos(angles), jnp.sin(angles)


def body(req_count, tp_count, tokens, norm_gain, w_query, w_kv, w_out, kv_cache, page_table, cached_len, span_len):
    fast = tp_count == 2 and req_count == 16 and w_out.shape[1] % 128 == 0 and w_kv.shape[1] == 4
    device = lax.axis_index("req")
    rank = lax.axis_index("tp")
    heads = w_kv.shape[1]
    dim = w_kv.shape[2] // 2
    group = w_query.shape[1] // dim // heads
    own_rows = tokens.shape[0]
    length = lax.dynamic_slice_in_dim(cached_len, device, 1)
    table = page_table[0]
    w_new = w_kv.reshape(w_kv.shape[0], -1)
    if fast:
        tables = cycle_tables(req_count)
        order = jnp.array(tables[3], jnp.int32)[device]
        swap = [(0, 1), (1, 0)]
        early = heads // 2
        cut = early * group * dim
        ring_first = Ring(w_query[:, :cut], tables)
        ring_second = Ring(jnp.concatenate([w_query[:, cut:], w_new], axis=1), tables)
        ring_out = Ring(w_out, tables)
        other = lax.ppermute(tokens, "tp", swap)
        whole = jnp.concatenate(
            [jnp.where(rank == 0, tokens, other), jnp.where(rank == 0, other, tokens)], axis=0
        )
        parts = 4
        state = ()
        for part in range(parts):
            state = prepare(kv_cache, table, length, part, parts, state)
            if part < parts - 1:
                ring_first.step()
                ring_second.step()
            else:
                first_chunks = ring_first.last()
                second_chunks = ring_second.last()
        keys, values = state
    else:
        order = jnp.zeros((1,), jnp.int32)
        early = 0
        gather = lambda array: lax.all_gather(array, "req", axis=0, tiled=True)
        second_chunks = [gather(jnp.concatenate([w_query, w_new], axis=1))]
        whole = lax.all_gather(tokens, "tp", axis=0, tiled=True)
        keys, values = prepare(kv_cache, table, length, 0, 1, ())
    hidden = whole.astype(jnp.float32)
    normed = (
        hidden * lax.rsqrt(jnp.mean(hidden * hidden, axis=-1, keepdims=True) + epsilon) * norm_gain
    ).astype(jnp.bfloat16)
    positions = length[0] + jnp.arange(normed.shape[0], dtype=jnp.int32)
    cosine, sines = rope_tables(positions, dim)
    queries = []
    if early:
        queries += project(normed, first_chunks, order, cosine, sines, early, 0, group, dim)
    late, new_keys, new_values = project(
        normed, second_chunks, order, cosine, sines, heads - early, heads, group, dim
    )
    queries.append(late)

    def attend_tile(tile, which, token):
        states = []
        for h in which:
            source, at = (queries[0], h) if h < early else (queries[-1], h - early)
            state, token = attend(at, h, tile, keys, values, source, token, span_len)
            states.append(state)
        return states, token

    def finish_tile(states, tile, chunks):
        return finish(
            states, tile, span_len, queries, new_keys, new_values, group, chunks, req_count
        )

    if not fast:
        rows = []
        for q in range(normed.shape[0] // token_tile):
            tile = jnp.full((1,), q, jnp.int32)
            states, _ = attend_tile(tile, range(heads), length)
            rows.append(finish_tile(states, tile, [])[0])
        gathered = lax.all_gather(w_out, "req", axis=1, tiled=True)
        partial = matmul(jnp.concatenate(rows, axis=0), gathered).astype(jnp.bfloat16)
        summed = lax.psum_scatter(partial, "tp", scatter_dimension=0, tiled=True)
        return (residual_scale * summed.astype(jnp.float32)).astype(jnp.bfloat16)
    theirs, ours = (1 - rank).reshape(1), rank.reshape(1)
    ring_out.step(ring_first.up)
    ring_out.step()
    ring_out.step()
    out_chunks = ring_out.last()
    sent_states, token = attend_tile(theirs, range(heads), length)
    kept_states, token = attend_tile(ours, range(heads // 2), token)
    sent, tile_token = finish_tile(sent_states, theirs, out_chunks)
    received = lax.ppermute(sent, "tp", swap)
    token = token + (tile_token - theirs)
    more, token = attend_tile(ours, range(heads // 2, heads), token)
    kept, _ = finish_tile(kept_states + more, ours, out_chunks)
    return combine(kept, received, order)


def solution(mesh):
    in_specs = (
        P(("req", "tp"), None),
        P(),
        P("req", "tp"),
        P("req", "tp", None),
        P("tp", "req"),
        P("req", None, "tp", None),
        P("req", None),
        P(),
        P("req"),
    )
    out_specs = P(("req", "tp"), None)
    program = functools.partial(body, mesh.shape["req"], mesh.shape["tp"])
    return jax.shard_map(
        program, mesh=mesh, in_specs=in_specs, out_specs=out_specs, check_vma=False
    )
```

```python
import functools

import jax
import jax.numpy as jnp
from jax import lax
from jax.experimental import pallas as pl
from jax.experimental.pallas import tpu as pltpu
from jax.sharding import PartitionSpec as P

epsilon = 1e-05
score_scale = 0.015625
residual_scale = 0.22
rope_base = 10000000.0
masked_score = -1e30
key_block = 1024
score_chunk = 256
value_chunk = 256
token_tile = 128


def matmul(a, b):
    return jnp.dot(a, b, preferred_element_type=jnp.float32)


def vmem():
    return pl.BlockSpec(memory_space=pltpu.VMEM)


def anywhere():
    return pl.BlockSpec(memory_space=pl.ANY)


def smem():
    return pl.BlockSpec(memory_space=pltpu.SMEM)


def params(mebibytes):
    return pltpu.CompilerParams(vmem_limit_bytes=mebibytes * 1024 * 1024)


def cycle_tables(count):
    depth = count // 4
    walk = [(z, 0) for z in range(depth)] + [(z, 1) for z in reversed(range(depth))]
    device = lambda chip, core: (chip[0] * 2 + chip[1]) * 2 + core
    length = len(walk)
    ahead = [
        (device(walk[k], c), device(walk[(k + 1) % length], c))
        for k in range(length)
        for c in range(2)
    ]
    back = [(b, a) for a, b in ahead]
    swap = [(i, i ^ 1) for i in range(count)]
    order = [None] * count
    for k in range(length):
        for c in range(2):
            row = []
            for step in range(length // 2):
                sources = [walk[(k - step) % length], walk[(k + step) % length]]
                for chip in sources[: 1 if step == 0 else 2]:
                    row += [device(chip, c), device(chip, 1 - c)]
            far = walk[(k + length // 2) % length]
            row += [device(far, c), device(far, 1 - c)]
            order[device(walk[k], c)] = row
    return ahead, back, swap, order


def after(value, *others):
    return lax.optimization_barrier((value,) + others)[0]


class Ring:
    def __init__(self, shard, tables):
        self.ahead, self.back, self.swap, self.order = tables
        self.length = len(self.order) // 2
        self.up = self.down = shard
        self.blocks = [shard, self.move(shard, self.swap)]

    def move(self, value, pairs):
        return lax.ppermute(value, "req", pairs)

    def step(self, *others):
        if others:
            self.up, self.down = lax.optimization_barrier((self.up, self.down) + others)[:2]
        self.up, self.down = self.move(self.up, self.ahead), self.move(self.down, self.back)
        self.blocks += [
            self.up,
            self.move(self.up, self.swap),
            self.down,
            self.move(self.down, self.swap),
        ]

    def last(self, upward, *others):
        if others:
            self.up, self.down = lax.optimization_barrier((self.up, self.down) + others)[:2]
        return self.move(self.up, self.ahead) if upward else self.move(self.down, self.back)

    def all(self, end, *others):
        if others:
            end = lax.optimization_barrier((end,) + others)[0]
        return self.blocks + [end, self.move(end, self.swap)]


def prepare_kernel(heads, page, width, pages_step, first_page, aliased, table_ref, length_ref, *refs):
    pages = refs[:pages_step]
    key_ref, value_ref, wide = refs[pages_step + aliased :]
    step = pl.program_id(0)
    half = width // 2
    rows = value_ref.shape[1]
    pick_row = lax.broadcasted_iota(jnp.int32, (rows, width), 0)
    pick_lane = lax.broadcasted_iota(jnp.int32, (rows, width), 1)
    pick = jnp.where(pick_lane == pick_row + half, 1.0, 0.0).astype(jnp.bfloat16)
    ones = jnp.where(lax.broadcasted_iota(jnp.int32, (rows, page), 0) == half, 1.0, 0.0)
    for i in range(pages_step):
        wide[i] = pages[i][0].astype(jnp.float32)
        first = (first_page + step * pages_step + i) * page
        position = first + lax.broadcasted_iota(jnp.int32, (page, width), 0)
        lane = lax.broadcasted_iota(jnp.int32, (page, width), 1)
        bias = jnp.where((lane == half) & (position >= length_ref[0]), masked_score, 0.0)
        for h in range(heads):
            rows_h = wide[i, pl.ds(h, page, stride=heads), :]
            key_ref[h, pl.ds(i * page, page), :] = jnp.where(lane < half, rows_h, bias).astype(
                jnp.bfloat16
            )
            turned = lax.dot_general(
                pick,
                rows_h.astype(jnp.bfloat16),
                (((1,), (1,)), ((), ())),
                preferred_element_type=jnp.float32,
            )
            value_ref[h, :, pl.ds(i * page, page)] = (turned + ones).astype(jnp.bfloat16)


def with_ones(turned):
    row = lax.broadcasted_iota(jnp.int32, (16, turned.shape[1]), 0)
    return jnp.concatenate([turned, jnp.where(row == 0, 1.0, 0.0)], axis=0)


def prepare(cache, table, length, part, parts, before):
    pages, page, heads, width = cache.shape
    pages_step = 4
    rows = width // 2 + 16
    total = table.shape[0]
    steps = total // pages_step // parts
    flat = cache.reshape(pages, page * heads, width)
    at = part * steps
    page_spec = lambda i: pl.BlockSpec(
        (1, page * heads, width), lambda j, t, n: (t[(at + j) * pages_step + i], 0, 0)
    )
    kept = [pl.BlockSpec(memory_space=pl.ANY)] * len(before)
    return pl.pallas_call(
        functools.partial(
            prepare_kernel, heads, page, width, pages_step, at * pages_step, len(before)
        ),
        grid_spec=pltpu.PrefetchScalarGridSpec(
            num_scalar_prefetch=2,
            grid=(steps,),
            in_specs=[page_spec(i) for i in range(pages_step)] + kept,
            out_specs=[
                pl.BlockSpec((heads, pages_step * page, width), lambda j, t, n: (0, at + j, 0)),
                pl.BlockSpec((heads, rows, pages_step * page), lambda j, t, n: (0, 0, at + j)),
            ],
            scratch_shapes=[pltpu.VMEM((pages_step, page * heads, width), jnp.float32)],
        ),
        out_shape=[
            jax.ShapeDtypeStruct((heads, total * page, width), jnp.bfloat16),
            jax.ShapeDtypeStruct((heads, rows, total * page), jnp.bfloat16),
        ],
        input_output_aliases={2 + pages_step + i: i for i in range(len(before))},
        cost_estimate=pl.CostEstimate(
            flops=0,
            bytes_accessed=3 * cache.size * cache.dtype.itemsize // parts,
            transcendentals=0,
        ),
        compiler_params=params(60),
        name="prepare",
    )(table, length, *([flat] * pages_step), *before)


def turn(pair, cosine, sines):
    half = pair.shape[0] // 2
    first, second = pair[:half], pair[half:]
    return jnp.concatenate(
        [first * cosine - second * sines, second * cosine + first * sines], axis=0
    )


def project_kernel(heads, new_heads, group, dim, blocks, order_ref, *refs):
    chunks = refs[:blocks]
    normed_hbm, cos_ref, sin_ref, query_ref = refs[blocks : blocks + 4]
    source, normed_ref, sems = refs[-3:]
    rows = source.shape[0] // blocks
    copies = [pltpu.make_async_copy(normed_hbm, normed_ref, sems.at[blocks])]
    for k in range(blocks):
        start = pl.multiple_of(order_ref[k] * rows, rows)
        copies.append(pltpu.make_async_copy(chunks[k], source.at[pl.ds(start, rows)], sems.at[k]))
    for copy in copies:
        copy.start()
    cosine, sines = cos_ref[...], sin_ref[...]
    tokens = cosine.shape[1]
    width = group * dim
    for copy in copies:
        copy.wait()
    normed = normed_ref[...]
    row = lax.broadcasted_iota(jnp.int32, (dim, group * token_tile), 0)
    one_row = jnp.where(row == 0, 1.0, 0.0).astype(jnp.bfloat16)
    for h in range(heads):
        turned = jnp.transpose(matmul(normed, source[:, pl.ds(h * width, width)]))
        for g in range(group):
            rotated = turn(turned[g * dim : (g + 1) * dim], cosine, sines).astype(jnp.bfloat16)
            scaled = (rotated.astype(jnp.float32) * score_scale).astype(jnp.bfloat16)
            for q in range(tokens // token_tile):
                query_ref[h, q, pl.ds(0, dim), pl.ds(g * token_tile, token_tile)] = scaled[
                    :, q * token_tile : (q + 1) * token_tile
                ]
        for q in range(tokens // token_tile):
            query_ref[h, q, pl.ds(dim, dim), :] = one_row
    for h in range(new_heads):
        key_ref, value_ref = refs[blocks + 4 : blocks + 6]
        at = heads * width + h * 2 * dim
        turned = jnp.transpose(matmul(normed, source[:, pl.ds(at, 2 * dim)]))
        keys = turn(turned[:dim], cosine, sines)
        padded = jnp.concatenate([keys, jnp.zeros_like(keys)], axis=0)
        key_ref[h] = jnp.transpose(padded).astype(jnp.bfloat16)
        value_ref[h] = with_ones(turned[dim:]).astype(jnp.bfloat16)


def project(normed, chunks, order, cosine, sines, heads, new_heads, group, dim):
    tokens, width = normed.shape
    columns = chunks[0].shape[1]
    outs = [(heads, tokens // token_tile, 2 * dim, group * token_tile)]
    if new_heads:
        outs += [(new_heads, tokens, 2 * dim), (new_heads, dim + 16, tokens)]
    return pl.pallas_call(
        functools.partial(project_kernel, heads, new_heads, group, dim, len(chunks)),
        in_specs=[smem()] + [anywhere()] * (len(chunks) + 1) + [vmem()] * 2,
        out_specs=[vmem()] * len(outs),
        out_shape=[jax.ShapeDtypeStruct(shape, jnp.bfloat16) for shape in outs],
        scratch_shapes=[
            pltpu.VMEM((width, columns), jnp.bfloat16),
            pltpu.VMEM((tokens, width), jnp.bfloat16),
            pltpu.SemaphoreType.DMA((len(chunks) + 1,)),
        ],
        cost_estimate=pl.CostEstimate(
            flops=2 * tokens * width * columns,
            bytes_accessed=2 * width * columns,
            transcendentals=0,
        ),
        compiler_params=params(60),
        name="project",
    )(order, *chunks, normed, cosine, sines)


def column_max(scores):
    return jnp.max(scores.reshape(scores.shape[0] // 8, 8, scores.shape[1]), axis=0)


def attend_kernel(
    heads,
    first_query,
    first_head,
    length_ref,
    span_ref,
    tile_ref,
    keys_hbm,
    values_hbm,
    queries_hbm,
    out_ref,
    token_ref,
    even,
    odd,
    keys_ref,
    values_ref,
    queries_ref,
    key_sems,
    value_sems,
    query_sems,
):
    lanes = out_ref.shape[2]
    length = length_ref[0]
    token_ref[0] = length
    q = tile_ref[0]
    pair = 2 * key_block
    sum_row = values_hbm.shape[1] - 16
    live = q * token_tile < span_ref[0]
    pairs = jnp.where(live, (length + pair - 1) // pair, 0)
    last_block = jnp.maximum(2 * pairs - 1, 0)
    row = lax.broadcasted_iota(jnp.int32, out_ref.shape[1:], 0)

    def key_copy(h, i):
        piece = pl.ds(pl.multiple_of(i * pair, pair), pair)
        return pltpu.make_async_copy(
            keys_hbm.at[first_head + h, piece], keys_ref.at[h & 1, piece], key_sems.at[h & 1, i]
        )

    def value_copy(h, i):
        piece = pl.ds(pl.multiple_of(i * pair, pair), pair)
        return pltpu.make_async_copy(
            values_hbm.at[first_head + h, :, piece],
            values_ref.at[h & 1, :, piece],
            value_sems.at[h & 1, i],
        )

    def query_copy(h):
        return pltpu.make_async_copy(
            queries_hbm.at[first_query + h, q], queries_ref.at[h], query_sems.at[h]
        )

    def fetch(h):
        def one(i, _):
            key_copy(h, i).start()
            value_copy(h, i).start()
            return 0

        lax.fori_loop(0, pairs, one, 0)

    def attend_head(h, _):
        query_copy(h).wait()
        key_copy(h, 0).wait()

        @pl.when(h + 1 < heads)
        def ahead():
            fetch(h + 1)

        key_ref, value_ref, query_ref = keys_ref.at[h & 1], values_ref.at[h & 1], queries_ref.at[h]
        def scores_of(block, c, target):
            start = pl.multiple_of(block * key_block + c * score_chunk, score_chunk)
            scores = matmul(key_ref[pl.ds(start, score_chunk), :], query_ref[...])
            target[pl.ds(c * score_chunk, score_chunk), :] = scores
            return column_max(scores)

        def half(block, following, current, target, state):
            maximum, top, total = state
            new_maximum = jnp.maximum(maximum, jnp.max(top, axis=0, keepdims=True))
            total = total * jnp.exp(maximum - new_maximum)
            next_top = None
            ratio = value_chunk // score_chunk
            parts = []
            for c in range(key_block // score_chunk):
                seen = scores_of(following, c, target)
                next_top = seen if next_top is None else jnp.maximum(next_top, seen)
                part = jnp.exp(current[pl.ds(c * score_chunk, score_chunk), :] - new_maximum)
                parts.append(part.astype(jnp.bfloat16))
                if len(parts) == ratio:
                    weights = parts[0] if ratio == 1 else jnp.concatenate(parts, axis=0)
                    start = block * key_block + (c + 1 - ratio) * score_chunk
                    start = pl.multiple_of(start, value_chunk)
                    total = total + matmul(value_ref[:, pl.ds(start, value_chunk)], weights)
                    parts = []
            return new_maximum, next_top, total

        def advance(i, state):
            @pl.when(i + 1 < pairs)
            def arrived():
                key_copy(h, i + 1).wait()

            value_copy(h, i).wait()
            block = 2 * i
            state = half(block, block + 1, even, odd, state)
            following = jnp.minimum(block + 2, last_block)
            return half(block + 1, following, odd, even, state)

        top = scores_of(0, 0, even)
        for c in range(1, key_block // score_chunk):
            top = jnp.maximum(top, scores_of(0, c, even))
        start = (
            jnp.full((1, lanes), masked_score, jnp.float32),
            top,
            jnp.zeros(row.shape, jnp.float32),
        )
        maximum, _, total = lax.fori_loop(0, pairs, advance, start)
        out_ref[h] = jnp.where(row == sum_row + 1, maximum, total)
        return 0

    @pl.when(pairs > 0)
    def work():
        for h in range(heads):
            query_copy(h).start()
        fetch(0)
        lax.fori_loop(0, heads, attend_head, 0)

    @pl.when(pairs == 0)
    def nothing():
        for h in range(heads):
            out_ref[h] = jnp.where(row == sum_row + 1, masked_score, 0.0)


def attend(heads, first_query, first_head, tile, keys, values, queries, token, valid):
    _, cached, width = keys.shape
    rows = values.shape[1]
    lanes = queries.shape[3]
    pieces = cached // (2 * key_block)
    return pl.pallas_call(
        functools.partial(attend_kernel, heads, first_query, first_head),
        in_specs=[smem()] * 3 + [anywhere()] * 3,
        out_specs=[vmem(), smem()],
        out_shape=[
            jax.ShapeDtypeStruct((heads, rows, lanes), jnp.float32),
            jax.ShapeDtypeStruct((1,), jnp.int32),
        ],
        scratch_shapes=[pltpu.VMEM((key_block, lanes), jnp.float32)] * 2
        + [
            pltpu.VMEM((2, cached, width), jnp.bfloat16),
            pltpu.VMEM((2, rows, cached), jnp.bfloat16),
            pltpu.VMEM((heads, width, lanes), jnp.bfloat16),
            pltpu.SemaphoreType.DMA((2, pieces)),
            pltpu.SemaphoreType.DMA((2, pieces)),
            pltpu.SemaphoreType.DMA((heads,)),
        ],
        cost_estimate=pl.CostEstimate(
            flops=8 * heads * cached * lanes * 2 * width,
            bytes_accessed=2 * heads * cached * 2 * width,
            transcendentals=heads * cached * lanes,
        ),
        compiler_params=params(60),
        name="attend",
    )(token, valid, tile, keys, values, queries)


def finish_head(q, valid, group, dim, state, query, new_key, new_value):
    lanes = query.shape[1]
    span = new_key.shape[0]
    scores = matmul(new_key, query)
    source = lax.broadcasted_iota(jnp.int32, (span, lanes), 0)
    lane = lax.broadcasted_iota(jnp.int32, (span, lanes), 1)
    position = q * token_tile + lax.rem(lane, token_tile)
    scores = jnp.where((source <= position) & (source < valid), scores, masked_score)
    cached_maximum = state[dim + 1 : dim + 2]
    maximum = jnp.maximum(jnp.max(column_max(scores), axis=0, keepdims=True), cached_maximum)
    weights = jnp.exp(scores - maximum).astype(jnp.bfloat16)
    total = state * jnp.exp(cached_maximum - maximum) + matmul(new_value, weights)
    result = total[:dim] / total[dim : dim + 1]
    row = q * token_tile + lax.broadcasted_iota(jnp.int32, (token_tile, 2 * dim), 0)
    pieces = []
    for g in range(0, group, 2):
        both = jnp.concatenate(
            [
                result[:, g * token_tile : (g + 1) * token_tile],
                result[:, (g + 1) * token_tile : (g + 2) * token_tile],
            ],
            axis=0,
        )
        pieces.append(jnp.where(row < valid, jnp.transpose(both), 0.0).astype(jnp.bfloat16))
    return pieces


def finish_kernel(heads, sets, group, dim, blocks, span_ref, tile_ref, *refs):
    states_hbm = refs[:sets]
    queries_hbm = refs[sets : sets + len(heads)]
    new_keys_hbm, new_values_hbm = refs[sets + len(heads) : sets + len(heads) + 2]
    at = sets + len(heads) + 2
    chunks = refs[at : at + blocks]
    out_ref, token_ref = refs[at + blocks : at + blocks + 2]
    states, queries, new_keys, new_values, weight, sems, weight_sems = refs[at + blocks + 2 :]
    q = tile_ref[0]
    token_ref[0] = q
    total = sum(heads)
    per_set = total // sets
    columns = weight.shape[1] // max(blocks, 1)
    copies = []
    for i in range(sets):
        copies.append((states_hbm[i], states.at[pl.ds(i * per_set, per_set)]))
    copies += [(new_keys_hbm, new_keys), (new_values_hbm, new_values)]
    source = [(which, h) for which, count in enumerate(heads) for h in range(count)]
    for h in range(total):
        which, place = source[h]
        copies.append((queries_hbm[which].at[place, q], queries.at[h]))
    copies = [pltpu.make_async_copy(a, b, sems.at[i]) for i, (a, b) in enumerate(copies)]
    loads = [
        pltpu.make_async_copy(
            chunks[k], weight.at[:, pl.ds(k * columns, columns)], weight_sems.at[k]
        )
        for k in range(blocks)
    ]
    for copy in copies + loads:
        copy.start()
    for copy in copies:
        copy.wait()
    pieces = []
    for h in range(total):
        pieces += finish_head(
            q, span_ref[0], group, dim, states[h], queries[h], new_keys[h], new_values[h]
        )
    attended = jnp.concatenate(pieces, axis=1)
    if blocks == 0:
        out_ref[...] = attended
        return
    for copy in loads:
        copy.wait()
    for k in range(0, blocks, 2):
        both = matmul(attended, weight[:, pl.ds(k * columns, 2 * columns)]).astype(jnp.bfloat16)
        out_ref[k] = both[:, :columns]
        out_ref[k + 1] = both[:, columns:]


def finish(states, tile, valid, queries, new_keys, new_values, group, chunks):
    heads = tuple(q.shape[0] for q in queries)
    total = sum(heads)
    rows, lanes = states[0].shape[1:]
    dim = rows - 16
    depth = total * group * dim
    blocks = len(chunks)
    columns = chunks[0].shape[1] if blocks else 128
    out = (blocks, token_tile, columns) if blocks else (token_tile, depth)
    return pl.pallas_call(
        functools.partial(finish_kernel, heads, len(states), group, dim, blocks),
        in_specs=[smem()] * 2 + [anywhere()] * (len(states) + len(queries) + 2 + blocks),
        out_specs=[vmem(), smem()],
        out_shape=[
            jax.ShapeDtypeStruct(out, jnp.bfloat16),
            jax.ShapeDtypeStruct((1,), jnp.int32),
        ],
        scratch_shapes=[
            pltpu.VMEM((total, rows, lanes), jnp.float32),
            pltpu.VMEM((total,) + queries[0].shape[2:], jnp.bfloat16),
            pltpu.VMEM(new_keys.shape, jnp.bfloat16),
            pltpu.VMEM(new_values.shape, jnp.bfloat16),
            pltpu.VMEM((depth if blocks else 16, max(blocks, 1) * columns), jnp.bfloat16),
            pltpu.SemaphoreType.DMA((len(states) + 2 + total,)),
            pltpu.SemaphoreType.DMA((max(blocks, 1),)),
        ],
        cost_estimate=pl.CostEstimate(
            flops=2 * token_tile * depth * columns * blocks,
            bytes_accessed=2 * depth * columns * blocks,
            transcendentals=0,
        ),
        compiler_params=params(60),
        name="finish",
    )(valid, tile, *states, *queries, new_keys, new_values, *chunks)


def combine_kernel(order_ref, own_ref, other_ref, out_ref):
    width = own_ref.shape[2]
    for k in range(own_ref.shape[0]):
        summed = own_ref[k].astype(jnp.float32) + other_ref[k].astype(jnp.float32)
        start = pl.multiple_of(order_ref[k] * width, width)
        out_ref[:, pl.ds(start, width)] = (residual_scale * summed).astype(jnp.bfloat16)


def combine(own, other, order):
    count, rows, columns = own.shape
    return pl.pallas_call(
        combine_kernel,
        in_specs=[smem(), vmem(), vmem()],
        out_specs=vmem(),
        out_shape=jax.ShapeDtypeStruct((rows, count * columns), jnp.bfloat16),
        compiler_params=params(60),
        name="combine",
    )(order, own, other)


def rope_tables(positions, dim):
    half_dim = dim // 2
    frequency = rope_base ** (-(jnp.arange(half_dim, dtype=jnp.float32) * 2.0 / dim))
    angles = positions.astype(jnp.float32)[None, :] * frequency[:, None]
    return jnp.cos(angles), jnp.sin(angles)


def body(req_count, tp_count, tokens, norm_gain, w_query, w_kv, w_out, kv_cache, page_table, cached_len, span_len):
    fast = tp_count == 2 and req_count == 16 and w_out.shape[1] % 128 == 0 and w_kv.shape[1] == 4
    device = lax.axis_index("req")
    rank = lax.axis_index("tp")
    heads = w_kv.shape[1]
    dim = w_kv.shape[2] // 2
    group = w_query.shape[1] // dim // heads
    own_rows = tokens.shape[0]
    length = lax.dynamic_slice_in_dim(cached_len, device, 1)
    table = page_table[0]
    w_new = w_kv.reshape(w_kv.shape[0], -1)
    if fast:
        tables = cycle_tables(req_count)
        order = jnp.array(tables[3], jnp.int32)[device]
        swap = [(0, 1), (1, 0)]
        early = heads // 2
        cut = early * group * dim
        ring_first = Ring(w_query[:, :cut], tables)
        ring_second = Ring(jnp.concatenate([w_query[:, cut:], w_new], axis=1), tables)
        ring_out = Ring(w_out, tables)
        other = lax.ppermute(tokens, "tp", swap)
        whole = jnp.concatenate(
            [jnp.where(rank == 0, tokens, other), jnp.where(rank == 0, other, tokens)], axis=0
        )
        parts = 2
        state = ()
        ring_first.step()
        ring_second.step()
        for part in range(parts):
            state = prepare(kv_cache, table, length, part, parts, state)
            ring_first.step()
            ring_second.step(state[0])
        first_chunks = ring_first.all(ring_first.last(True))
        keys, values = state
    else:
        order = jnp.zeros((1,), jnp.int32)
        early = 0
        gather = lambda array: lax.all_gather(array, "req", axis=0, tiled=True)
        second_chunks = [gather(jnp.concatenate([w_query, w_new], axis=1))]
        whole = lax.all_gather(tokens, "tp", axis=0, tiled=True)
        keys, values = prepare(kv_cache, table, length, 0, 1, ())
    hidden = whole.astype(jnp.float32)
    normed = (
        hidden * lax.rsqrt(jnp.mean(hidden * hidden, axis=-1, keepdims=True) + epsilon) * norm_gain
    ).astype(jnp.bfloat16)
    positions = length[0] + jnp.arange(normed.shape[0], dtype=jnp.int32)
    cosine, sines = rope_tables(positions, dim)
    queries = []

    def attend_tile(tile, source, count, first, token):
        return attend(count, 0, first, tile, keys, values, source, token, span_len)

    def finish_tile(states, tile, chunks):
        return finish(states, tile, span_len, queries, new_keys, new_values, group, chunks)

    if not fast:
        late, new_keys, new_values = project(
            normed, second_chunks, order, cosine, sines, heads, heads, group, dim
        )
        queries.append(late)
        rows = []
        for q in range(normed.shape[0] // token_tile):
            tile = jnp.full((1,), q, jnp.int32)
            state, _ = attend_tile(tile, late, heads, 0, length)
            rows.append(finish_tile([state], tile, [])[0])
        gathered = lax.all_gather(w_out, "req", axis=1, tiled=True)
        partial = matmul(jnp.concatenate(rows, axis=0), gathered).astype(jnp.bfloat16)
        summed = lax.psum_scatter(partial, "tp", scatter_dimension=0, tiled=True)
        return (residual_scale * summed.astype(jnp.float32)).astype(jnp.bfloat16)
    theirs, ours = (1 - rank).reshape(1), rank.reshape(1)
    ring_out.step(ring_first.up)
    soon = project(normed, first_chunks, order, cosine, sines, early, 0, group, dim)[0]
    second_end = ring_second.last(False, soon)
    ring_out.step(soon)
    sent_first, token = attend_tile(theirs, soon, early, 0, length)
    second_chunks = ring_second.all(second_end, sent_first)
    ring_out.step(sent_first)
    late, new_keys, new_values = project(
        normed, second_chunks, order, cosine, sines, heads - early, heads, group, dim
    )
    queries += [soon, late]
    sent_second, token = attend_tile(theirs, late, heads - early, early, token)
    out_end = ring_out.last(True, sent_second)
    kept_first, token = attend_tile(ours, soon, early, 0, token)
    out_chunks = ring_out.all(out_end, kept_first)
    sent, tile_token = finish_tile([sent_first, sent_second], theirs, out_chunks)
    received = lax.ppermute(sent, "tp", swap)
    token = token + (tile_token - theirs)
    kept_second, token = attend_tile(ours, late, heads - early, early, token)
    kept, _ = finish_tile([kept_first, kept_second], ours, out_chunks)
    return combine(kept, received, order)


def solution(mesh):
    in_specs = (
        P(("req", "tp"), None),
        P(),
        P("req", "tp"),
        P("req", "tp", None),
        P("tp", "req"),
        P("req", None, "tp", None),
        P("req", None),
        P(),
        P("req"),
    )
    out_specs = P(("req", "tp"), None)
    program = functools.partial(body, mesh.shape["req"], mesh.shape["tp"])
    return jax.shard_map(
        program, mesh=mesh, in_specs=in_specs, out_specs=out_specs, check_vma=False
    )
```

```python
import functools

import jax
import jax.numpy as jnp
from jax import lax
from jax.experimental import pallas as pl
from jax.experimental.pallas import tpu as pltpu
from jax.sharding import PartitionSpec as P

epsilon = 1e-05
score_scale = 0.015625
residual_scale = 0.22
rope_base = 10000000.0
masked_score = -1e30
key_block = 1024
score_chunk = 256
value_chunk = 256
token_tile = 128


def matmul(a, b):
    return jnp.dot(a, b, preferred_element_type=jnp.float32)


def vmem():
    return pl.BlockSpec(memory_space=pltpu.VMEM)


def anywhere():
    return pl.BlockSpec(memory_space=pl.ANY)


def smem():
    return pl.BlockSpec(memory_space=pltpu.SMEM)


def params(mebibytes):
    return pltpu.CompilerParams(vmem_limit_bytes=mebibytes * 1024 * 1024)


def cycle_tables(count):
    depth = count // 4
    walk = [(z, 0) for z in range(depth)] + [(z, 1) for z in reversed(range(depth))]
    device = lambda chip, core: (chip[0] * 2 + chip[1]) * 2 + core
    length = len(walk)
    ahead = [
        (device(walk[k], c), device(walk[(k + 1) % length], c))
        for k in range(length)
        for c in range(2)
    ]
    back = [(b, a) for a, b in ahead]
    swap = [(i, i ^ 1) for i in range(count)]
    order = [None] * count
    for k in range(length):
        for c in range(2):
            row = []
            for step in range(length // 2):
                sources = [walk[(k - step) % length], walk[(k + step) % length]]
                for chip in sources[: 1 if step == 0 else 2]:
                    row += [device(chip, c), device(chip, 1 - c)]
            far = walk[(k + length // 2) % length]
            row += [device(far, c), device(far, 1 - c)]
            order[device(walk[k], c)] = row
    return ahead, back, swap, order


def after(value, *others):
    return lax.optimization_barrier((value,) + others)[0]


def assemble_kernel(*refs):
    *blocks, out_ref, sems = refs
    rows = blocks[0].shape[0]
    copies = [
        pltpu.make_async_copy(block, out_ref.at[pl.ds(k * rows, rows)], sems.at[k])
        for k, block in enumerate(blocks)
    ]
    for copy in copies:
        copy.start()
    for copy in copies:
        copy.wait()


def assemble(blocks):
    rows, columns = blocks[0].shape
    return pl.pallas_call(
        assemble_kernel,
        in_specs=[anywhere()] * len(blocks),
        out_specs=vmem(),
        out_shape=jax.ShapeDtypeStruct((len(blocks) * rows, columns), blocks[0].dtype),
        scratch_shapes=[pltpu.SemaphoreType.DMA((len(blocks),))],
        cost_estimate=pl.CostEstimate(
            flops=0, bytes_accessed=4 * len(blocks) * rows * columns, transcendentals=0
        ),
        compiler_params=params(60),
        name="assemble",
    )(*blocks)


class Ring:
    def __init__(self, shard, tables):
        self.ahead, self.back, self.swap, self.order = tables
        self.up = self.down = shard
        self.blocks = [shard]

    def move(self, value, pairs):
        return lax.ppermute(value, "req", pairs)

    def step(self, *others):
        if others:
            self.up, self.down = lax.optimization_barrier((self.up, self.down) + others)[:2]
        self.up, self.down = self.move(self.up, self.ahead), self.move(self.down, self.back)
        self.blocks += [self.up, self.down]

    def last(self, upward, *others):
        if others:
            self.up, self.down = lax.optimization_barrier((self.up, self.down) + others)[:2]
        return self.move(self.up, self.ahead) if upward else self.move(self.down, self.back)

    def partner(self, *others):
        blocks = self.blocks
        if others:
            blocks = list(lax.optimization_barrier(tuple(blocks) + others)[: len(blocks)])
        return self.move(assemble(blocks), self.swap)

    def all(self, end, partner):
        return self.blocks + [end, partner, self.move(end, self.swap)]


def chunk_sources(refs):
    *own, partner, end = refs
    rows = own[0].shape[0]
    sources = []
    for k, block in enumerate(own):
        at = partner.at[pl.ds(k * rows, rows)] if k < len(own) - 1 else end
        sources += [block, at]
    return sources


def prepare_kernel(heads, page, width, pages_step, first_page, aliased, table_ref, length_ref, *refs):
    pages = refs[:pages_step]
    key_ref, value_ref, wide = refs[pages_step + aliased :]
    step = pl.program_id(0)
    half = width // 2
    rows = value_ref.shape[1]
    pick_row = lax.broadcasted_iota(jnp.int32, (rows, width), 0)
    pick_lane = lax.broadcasted_iota(jnp.int32, (rows, width), 1)
    pick = jnp.where(pick_lane == pick_row + half, 1.0, 0.0).astype(jnp.bfloat16)
    ones = jnp.where(lax.broadcasted_iota(jnp.int32, (rows, page), 0) == half, 1.0, 0.0)
    for i in range(pages_step):
        wide[i] = pages[i][0].astype(jnp.float32)
        first = (first_page + step * pages_step + i) * page
        position = first + lax.broadcasted_iota(jnp.int32, (page, width), 0)
        lane = lax.broadcasted_iota(jnp.int32, (page, width), 1)
        bias = jnp.where((lane == half) & (position >= length_ref[0]), masked_score, 0.0)
        for h in range(heads):
            rows_h = wide[i, pl.ds(h, page, stride=heads), :]
            key_ref[h, pl.ds(i * page, page), :] = jnp.where(lane < half, rows_h, bias).astype(
                jnp.bfloat16
            )
            turned = lax.dot_general(
                pick,
                rows_h.astype(jnp.bfloat16),
                (((1,), (1,)), ((), ())),
                preferred_element_type=jnp.float32,
            )
            value_ref[h, :, pl.ds(i * page, page)] = (turned + ones).astype(jnp.bfloat16)


def with_ones(turned):
    row = lax.broadcasted_iota(jnp.int32, (16, turned.shape[1]), 0)
    return jnp.concatenate([turned, jnp.where(row == 0, 1.0, 0.0)], axis=0)


def prepare(cache, table, length, part, parts, before):
    pages, page, heads, width = cache.shape
    pages_step = 4
    rows = width // 2 + 16
    total = table.shape[0]
    steps = total // pages_step // parts
    flat = cache.reshape(pages, page * heads, width)
    at = part * steps
    page_spec = lambda i: pl.BlockSpec(
        (1, page * heads, width), lambda j, t, n: (t[(at + j) * pages_step + i], 0, 0)
    )
    kept = [pl.BlockSpec(memory_space=pl.ANY)] * len(before)
    return pl.pallas_call(
        functools.partial(
            prepare_kernel, heads, page, width, pages_step, at * pages_step, len(before)
        ),
        grid_spec=pltpu.PrefetchScalarGridSpec(
            num_scalar_prefetch=2,
            grid=(steps,),
            in_specs=[page_spec(i) for i in range(pages_step)] + kept,
            out_specs=[
                pl.BlockSpec((heads, pages_step * page, width), lambda j, t, n: (0, at + j, 0)),
                pl.BlockSpec((heads, rows, pages_step * page), lambda j, t, n: (0, 0, at + j)),
            ],
            scratch_shapes=[pltpu.VMEM((pages_step, page * heads, width), jnp.float32)],
        ),
        out_shape=[
            jax.ShapeDtypeStruct((heads, total * page, width), jnp.bfloat16),
            jax.ShapeDtypeStruct((heads, rows, total * page), jnp.bfloat16),
        ],
        input_output_aliases={2 + pages_step + i: i for i in range(len(before))},
        cost_estimate=pl.CostEstimate(
            flops=0,
            bytes_accessed=3 * cache.size * cache.dtype.itemsize // parts,
            transcendentals=0,
        ),
        compiler_params=params(60),
        name="prepare",
    )(table, length, *([flat] * pages_step), *before)


def turn(pair, cosine, sines):
    half = pair.shape[0] // 2
    first, second = pair[:half], pair[half:]
    return jnp.concatenate(
        [first * cosine - second * sines, second * cosine + first * sines], axis=0
    )


def project_kernel(heads, new_heads, group, dim, blocks, order_ref, *refs):
    chunks = refs[:blocks]
    normed_hbm, cos_ref, sin_ref, query_ref = refs[blocks : blocks + 4]
    source, normed_ref, sems = refs[-3:]
    sources = chunks if blocks == 1 else chunk_sources(chunks)
    count = len(sources)
    rows = source.shape[0] // count
    copies = [pltpu.make_async_copy(normed_hbm, normed_ref, sems.at[count])]
    for k in range(count):
        start = pl.multiple_of(order_ref[k] * rows, rows)
        copies.append(pltpu.make_async_copy(sources[k], source.at[pl.ds(start, rows)], sems.at[k]))
    for copy in copies:
        copy.start()
    cosine, sines = cos_ref[...], sin_ref[...]
    tokens = cosine.shape[1]
    width = group * dim
    for copy in copies:
        copy.wait()
    normed = normed_ref[...]
    row = lax.broadcasted_iota(jnp.int32, (dim, group * token_tile), 0)
    one_row = jnp.where(row == 0, 1.0, 0.0).astype(jnp.bfloat16)
    for h in range(heads):
        turned = jnp.transpose(matmul(normed, source[:, pl.ds(h * width, width)]))
        for g in range(group):
            rotated = turn(turned[g * dim : (g + 1) * dim], cosine, sines).astype(jnp.bfloat16)
            scaled = (rotated.astype(jnp.float32) * score_scale).astype(jnp.bfloat16)
            for q in range(tokens // token_tile):
                query_ref[h, q, pl.ds(0, dim), pl.ds(g * token_tile, token_tile)] = scaled[
                    :, q * token_tile : (q + 1) * token_tile
                ]
        for q in range(tokens // token_tile):
            query_ref[h, q, pl.ds(dim, dim), :] = one_row
    for h in range(new_heads):
        key_ref, value_ref = refs[blocks + 4 : blocks + 6]
        at = heads * width + h * 2 * dim
        turned = jnp.transpose(matmul(normed, source[:, pl.ds(at, 2 * dim)]))
        keys = turn(turned[:dim], cosine, sines)
        padded = jnp.concatenate([keys, jnp.zeros_like(keys)], axis=0)
        key_ref[h] = jnp.transpose(padded).astype(jnp.bfloat16)
        value_ref[h] = with_ones(turned[dim:]).astype(jnp.bfloat16)


def project(normed, chunks, order, cosine, sines, heads, new_heads, group, dim):
    tokens, width = normed.shape
    columns = chunks[0].shape[1]
    outs = [(heads, tokens // token_tile, 2 * dim, group * token_tile)]
    if new_heads:
        outs += [(new_heads, tokens, 2 * dim), (new_heads, dim + 16, tokens)]
    return pl.pallas_call(
        functools.partial(project_kernel, heads, new_heads, group, dim, len(chunks)),
        in_specs=[smem()] + [anywhere()] * (len(chunks) + 1) + [vmem()] * 2,
        out_specs=[vmem()] * len(outs),
        out_shape=[jax.ShapeDtypeStruct(shape, jnp.bfloat16) for shape in outs],
        scratch_shapes=[
            pltpu.VMEM((width, columns), jnp.bfloat16),
            pltpu.VMEM((tokens, width), jnp.bfloat16),
            pltpu.SemaphoreType.DMA((order.shape[0] + 1,)),
        ],
        cost_estimate=pl.CostEstimate(
            flops=2 * tokens * width * columns,
            bytes_accessed=2 * width * columns,
            transcendentals=0,
        ),
        compiler_params=params(60),
        name="project",
    )(order, *chunks, normed, cosine, sines)


def column_max(scores):
    return jnp.max(scores.reshape(scores.shape[0] // 8, 8, scores.shape[1]), axis=0)


def attend_kernel(
    heads,
    first_query,
    first_head,
    length_ref,
    span_ref,
    tile_ref,
    keys_hbm,
    values_hbm,
    queries_hbm,
    out_ref,
    token_ref,
    even,
    odd,
    keys_ref,
    values_ref,
    queries_ref,
    key_sems,
    value_sems,
    query_sems,
):
    lanes = out_ref.shape[2]
    length = length_ref[0]
    token_ref[0] = length
    q = tile_ref[0]
    pair = 2 * key_block
    sum_row = values_hbm.shape[1] - 16
    live = q * token_tile < span_ref[0]
    pairs = jnp.where(live, (length + pair - 1) // pair, 0)
    last_block = jnp.maximum(2 * pairs - 1, 0)
    row = lax.broadcasted_iota(jnp.int32, out_ref.shape[1:], 0)

    def key_copy(h, i):
        piece = pl.ds(pl.multiple_of(i * pair, pair), pair)
        return pltpu.make_async_copy(
            keys_hbm.at[first_head + h, piece], keys_ref.at[h & 1, piece], key_sems.at[h & 1, i]
        )

    def value_copy(h, i):
        piece = pl.ds(pl.multiple_of(i * pair, pair), pair)
        return pltpu.make_async_copy(
            values_hbm.at[first_head + h, :, piece],
            values_ref.at[h & 1, :, piece],
            value_sems.at[h & 1, i],
        )

    def query_copy(h):
        return pltpu.make_async_copy(
            queries_hbm.at[first_query + h, q], queries_ref.at[h], query_sems.at[h]
        )

    def fetch(h):
        def one(i, _):
            key_copy(h, i).start()
            value_copy(h, i).start()
            return 0

        lax.fori_loop(0, pairs, one, 0)

    def attend_head(h, _):
        query_copy(h).wait()
        key_copy(h, 0).wait()

        @pl.when(h + 1 < heads)
        def ahead():
            fetch(h + 1)

        key_ref, value_ref, query_ref = keys_ref.at[h & 1], values_ref.at[h & 1], queries_ref.at[h]
        def scores_of(block, c, target):
            start = pl.multiple_of(block * key_block + c * score_chunk, score_chunk)
            scores = matmul(key_ref[pl.ds(start, score_chunk), :], query_ref[...])
            target[pl.ds(c * score_chunk, score_chunk), :] = scores
            return column_max(scores)

        def half(block, following, current, target, state):
            maximum, top, total = state
            new_maximum = jnp.maximum(maximum, jnp.max(top, axis=0, keepdims=True))
            total = total * jnp.exp(maximum - new_maximum)
            next_top = None
            ratio = value_chunk // score_chunk
            parts = []
            for c in range(key_block // score_chunk):
                seen = scores_of(following, c, target)
                next_top = seen if next_top is None else jnp.maximum(next_top, seen)
                part = jnp.exp(current[pl.ds(c * score_chunk, score_chunk), :] - new_maximum)
                parts.append(part.astype(jnp.bfloat16))
                if len(parts) == ratio:
                    weights = parts[0] if ratio == 1 else jnp.concatenate(parts, axis=0)
                    start = block * key_block + (c + 1 - ratio) * score_chunk
                    start = pl.multiple_of(start, value_chunk)
                    total = total + matmul(value_ref[:, pl.ds(start, value_chunk)], weights)
                    parts = []
            return new_maximum, next_top, total

        def advance(i, state):
            @pl.when(i + 1 < pairs)
            def arrived():
                key_copy(h, i + 1).wait()

            value_copy(h, i).wait()
            block = 2 * i
            state = half(block, block + 1, even, odd, state)
            following = jnp.minimum(block + 2, last_block)
            return half(block + 1, following, odd, even, state)

        top = scores_of(0, 0, even)
        for c in range(1, key_block // score_chunk):
            top = jnp.maximum(top, scores_of(0, c, even))
        start = (
            jnp.full((1, lanes), masked_score, jnp.float32),
            top,
            jnp.zeros(row.shape, jnp.float32),
        )
        maximum, _, total = lax.fori_loop(0, pairs, advance, start)
        out_ref[h] = jnp.where(row == sum_row + 1, maximum, total)
        return 0

    @pl.when(pairs > 0)
    def work():
        for h in range(heads):
            query_copy(h).start()
        fetch(0)
        lax.fori_loop(0, heads, attend_head, 0)

    @pl.when(pairs == 0)
    def nothing():
        for h in range(heads):
            out_ref[h] = jnp.where(row == sum_row + 1, masked_score, 0.0)


def attend(heads, first_query, first_head, tile, keys, values, queries, token, valid):
    _, cached, width = keys.shape
    rows = values.shape[1]
    lanes = queries.shape[3]
    pieces = cached // (2 * key_block)
    return pl.pallas_call(
        functools.partial(attend_kernel, heads, first_query, first_head),
        in_specs=[smem()] * 3 + [anywhere()] * 3,
        out_specs=[vmem(), smem()],
        out_shape=[
            jax.ShapeDtypeStruct((heads, rows, lanes), jnp.float32),
            jax.ShapeDtypeStruct((1,), jnp.int32),
        ],
        scratch_shapes=[pltpu.VMEM((key_block, lanes), jnp.float32)] * 2
        + [
            pltpu.VMEM((2, cached, width), jnp.bfloat16),
            pltpu.VMEM((2, rows, cached), jnp.bfloat16),
            pltpu.VMEM((heads, width, lanes), jnp.bfloat16),
            pltpu.SemaphoreType.DMA((2, pieces)),
            pltpu.SemaphoreType.DMA((2, pieces)),
            pltpu.SemaphoreType.DMA((heads,)),
        ],
        cost_estimate=pl.CostEstimate(
            flops=8 * heads * cached * lanes * 2 * width,
            bytes_accessed=2 * heads * cached * 2 * width,
            transcendentals=heads * cached * lanes,
        ),
        compiler_params=params(60),
        name="attend",
    )(token, valid, tile, keys, values, queries)


def finish_head(q, valid, group, dim, state, query, new_key, new_value):
    lanes = query.shape[1]
    span = new_key.shape[0]
    scores = matmul(new_key, query)
    source = lax.broadcasted_iota(jnp.int32, (span, lanes), 0)
    lane = lax.broadcasted_iota(jnp.int32, (span, lanes), 1)
    position = q * token_tile + lax.rem(lane, token_tile)
    scores = jnp.where((source <= position) & (source < valid), scores, masked_score)
    cached_maximum = state[dim + 1 : dim + 2]
    maximum = jnp.maximum(jnp.max(column_max(scores), axis=0, keepdims=True), cached_maximum)
    weights = jnp.exp(scores - maximum).astype(jnp.bfloat16)
    total = state * jnp.exp(cached_maximum - maximum) + matmul(new_value, weights)
    result = total[:dim] / total[dim : dim + 1]
    row = q * token_tile + lax.broadcasted_iota(jnp.int32, (token_tile, 2 * dim), 0)
    pieces = []
    for g in range(0, group, 2):
        both = jnp.concatenate(
            [
                result[:, g * token_tile : (g + 1) * token_tile],
                result[:, (g + 1) * token_tile : (g + 2) * token_tile],
            ],
            axis=0,
        )
        pieces.append(jnp.where(row < valid, jnp.transpose(both), 0.0).astype(jnp.bfloat16))
    return pieces


def finish_kernel(heads, sets, group, dim, blocks, span_ref, tile_ref, *refs):
    states_hbm = refs[:sets]
    queries_hbm = refs[sets : sets + len(heads)]
    new_keys_hbm, new_values_hbm = refs[sets + len(heads) : sets + len(heads) + 2]
    at = sets + len(heads) + 2
    chunks = refs[at : at + blocks]
    out_ref, token_ref = refs[at + blocks : at + blocks + 2]
    states, queries, new_keys, new_values, weight, sems, weight_sems = refs[at + blocks + 2 :]
    q = tile_ref[0]
    token_ref[0] = q
    total = sum(heads)
    per_set = total // sets
    chunks = chunk_sources(chunks) if blocks else []
    count = len(chunks)
    columns = weight.shape[1] // max(count, 1)
    copies = []
    for i in range(sets):
        copies.append((states_hbm[i], states.at[pl.ds(i * per_set, per_set)]))
    copies += [(new_keys_hbm, new_keys), (new_values_hbm, new_values)]
    source = [(which, h) for which, count in enumerate(heads) for h in range(count)]
    for h in range(total):
        which, place = source[h]
        copies.append((queries_hbm[which].at[place, q], queries.at[h]))
    copies = [pltpu.make_async_copy(a, b, sems.at[i]) for i, (a, b) in enumerate(copies)]
    loads = [
        pltpu.make_async_copy(
            chunks[k], weight.at[:, pl.ds(k * columns, columns)], weight_sems.at[k]
        )
        for k in range(count)
    ]
    for copy in copies + loads:
        copy.start()
    for copy in copies:
        copy.wait()
    pieces = []
    for h in range(total):
        pieces += finish_head(
            q, span_ref[0], group, dim, states[h], queries[h], new_keys[h], new_values[h]
        )
    attended = jnp.concatenate(pieces, axis=1)
    if blocks == 0:
        out_ref[...] = attended
        return
    for copy in loads:
        copy.wait()
    for k in range(0, count, 2):
        both = matmul(attended, weight[:, pl.ds(k * columns, 2 * columns)]).astype(jnp.bfloat16)
        out_ref[k] = both[:, :columns]
        out_ref[k + 1] = both[:, columns:]


def finish(states, tile, valid, queries, new_keys, new_values, group, chunks):
    heads = tuple(q.shape[0] for q in queries)
    total = sum(heads)
    rows, lanes = states[0].shape[1:]
    dim = rows - 16
    depth = total * group * dim
    blocks = len(chunks)
    count = 2 * (blocks - 2) if blocks else 0
    columns = chunks[0].shape[1] if blocks else 128
    out = (count, token_tile, columns) if blocks else (token_tile, depth)
    return pl.pallas_call(
        functools.partial(finish_kernel, heads, len(states), group, dim, blocks),
        in_specs=[smem()] * 2 + [anywhere()] * (len(states) + len(queries) + 2 + blocks),
        out_specs=[vmem(), smem()],
        out_shape=[
            jax.ShapeDtypeStruct(out, jnp.bfloat16),
            jax.ShapeDtypeStruct((1,), jnp.int32),
        ],
        scratch_shapes=[
            pltpu.VMEM((total, rows, lanes), jnp.float32),
            pltpu.VMEM((total,) + queries[0].shape[2:], jnp.bfloat16),
            pltpu.VMEM(new_keys.shape, jnp.bfloat16),
            pltpu.VMEM(new_values.shape, jnp.bfloat16),
            pltpu.VMEM((depth if blocks else 16, max(count, 1) * columns), jnp.bfloat16),
            pltpu.SemaphoreType.DMA((len(states) + 2 + total,)),
            pltpu.SemaphoreType.DMA((max(count, 1),)),
        ],
        cost_estimate=pl.CostEstimate(
            flops=2 * token_tile * depth * columns * count,
            bytes_accessed=2 * depth * columns * count,
            transcendentals=0,
        ),
        compiler_params=params(60),
        name="finish",
    )(valid, tile, *states, *queries, new_keys, new_values, *chunks)


def combine_kernel(order_ref, own_ref, other_ref, out_ref):
    width = own_ref.shape[2]
    for k in range(own_ref.shape[0]):
        summed = own_ref[k].astype(jnp.float32) + other_ref[k].astype(jnp.float32)
        start = pl.multiple_of(order_ref[k] * width, width)
        out_ref[:, pl.ds(start, width)] = (residual_scale * summed).astype(jnp.bfloat16)


def combine(own, other, order):
    count, rows, columns = own.shape
    return pl.pallas_call(
        combine_kernel,
        in_specs=[smem(), vmem(), vmem()],
        out_specs=vmem(),
        out_shape=jax.ShapeDtypeStruct((rows, count * columns), jnp.bfloat16),
        compiler_params=params(60),
        name="combine",
    )(order, own, other)


def rope_tables(positions, dim):
    half_dim = dim // 2
    frequency = rope_base ** (-(jnp.arange(half_dim, dtype=jnp.float32) * 2.0 / dim))
    angles = positions.astype(jnp.float32)[None, :] * frequency[:, None]
    return jnp.cos(angles), jnp.sin(angles)


def body(req_count, tp_count, tokens, norm_gain, w_query, w_kv, w_out, kv_cache, page_table, cached_len, span_len):
    fast = tp_count == 2 and req_count == 16 and w_out.shape[1] % 128 == 0 and w_kv.shape[1] == 4
    device = lax.axis_index("req")
    rank = lax.axis_index("tp")
    heads = w_kv.shape[1]
    dim = w_kv.shape[2] // 2
    group = w_query.shape[1] // dim // heads
    own_rows = tokens.shape[0]
    length = lax.dynamic_slice_in_dim(cached_len, device, 1)
    table = page_table[0]
    w_new = w_kv.reshape(w_kv.shape[0], -1)
    if fast:
        tables = cycle_tables(req_count)
        order = jnp.array(tables[3], jnp.int32)[device]
        swap = [(0, 1), (1, 0)]
        early = heads // 2
        cut = early * group * dim
        ring_first = Ring(w_query[:, :cut], tables)
        ring_second = Ring(jnp.concatenate([w_query[:, cut:], w_new], axis=1), tables)
        ring_out = Ring(w_out, tables)
        other = lax.ppermute(tokens, "tp", swap)
        whole = jnp.concatenate(
            [jnp.where(rank == 0, tokens, other), jnp.where(rank == 0, other, tokens)], axis=0
        )
        parts = 2
        state = ()
        ring_first.step()
        ring_second.step()
        for part in range(parts):
            state = prepare(kv_cache, table, length, part, parts, state)
            ring_first.step()
            ring_second.step(state[0])
        first_end = ring_first.last(True)
        first_chunks = ring_first.all(first_end, ring_first.partner())
        ring_out.step(first_end)
        keys, values = state
    else:
        order = jnp.zeros((1,), jnp.int32)
        early = 0
        gather = lambda array: lax.all_gather(array, "req", axis=0, tiled=True)
        second_chunks = [gather(jnp.concatenate([w_query, w_new], axis=1))]
        whole = lax.all_gather(tokens, "tp", axis=0, tiled=True)
        keys, values = prepare(kv_cache, table, length, 0, 1, ())
    hidden = whole.astype(jnp.float32)
    normed = (
        hidden * lax.rsqrt(jnp.mean(hidden * hidden, axis=-1, keepdims=True) + epsilon) * norm_gain
    ).astype(jnp.bfloat16)
    positions = length[0] + jnp.arange(normed.shape[0], dtype=jnp.int32)
    cosine, sines = rope_tables(positions, dim)
    queries = []

    def attend_tile(tile, source, count, first, token):
        return attend(count, 0, first, tile, keys, values, source, token, span_len)

    def finish_tile(states, tile, chunks):
        return finish(states, tile, span_len, queries, new_keys, new_values, group, chunks)

    if not fast:
        late, new_keys, new_values = project(
            normed, second_chunks, order, cosine, sines, heads, heads, group, dim
        )
        queries.append(late)
        rows = []
        for q in range(normed.shape[0] // token_tile):
            tile = jnp.full((1,), q, jnp.int32)
            state, _ = attend_tile(tile, late, heads, 0, length)
            rows.append(finish_tile([state], tile, [])[0])
        gathered = lax.all_gather(w_out, "req", axis=1, tiled=True)
        partial = matmul(jnp.concatenate(rows, axis=0), gathered).astype(jnp.bfloat16)
        summed = lax.psum_scatter(partial, "tp", scatter_dimension=0, tiled=True)
        return (residual_scale * summed.astype(jnp.float32)).astype(jnp.bfloat16)
    theirs, ours = (1 - rank).reshape(1), rank.reshape(1)
    soon = project(normed, first_chunks, order, cosine, sines, early, 0, group, dim)[0]
    second_end = ring_second.last(False, soon)
    ring_out.step(soon)
    sent_first, token = attend_tile(theirs, soon, early, 0, length)
    second_chunks = ring_second.all(after(second_end, sent_first), ring_second.partner(sent_first))
    ring_out.step(sent_first)
    kept_first, token = attend_tile(ours, soon, early, 0, token)
    late, new_keys, new_values = project(
        normed, second_chunks, order, cosine, sines, heads - early, heads, group, dim
    )
    queries += [soon, late]
    out_end = ring_out.last(True, kept_first)
    out_partner = ring_out.partner(kept_first)
    sent_second, token = attend_tile(theirs, late, heads - early, early, token)
    out_chunks = ring_out.all(after(out_end, sent_second), out_partner)
    sent, tile_token = finish_tile([sent_first, sent_second], theirs, out_chunks)
    received = lax.ppermute(sent, "tp", swap)
    token = token + (tile_token - theirs)
    kept_second, token = attend_tile(ours, late, heads - early, early, token)
    kept, _ = finish_tile([kept_first, kept_second], ours, out_chunks)
    return combine(kept, received, order)


def solution(mesh):
    in_specs = (
        P(("req", "tp"), None),
        P(),
        P("req", "tp"),
        P("req", "tp", None),
        P("tp", "req"),
        P("req", None, "tp", None),
        P("req", None),
        P(),
        P("req"),
    )
    out_specs = P(("req", "tp"), None)
    program = functools.partial(body, mesh.shape["req"], mesh.shape["tp"])
    return jax.shard_map(
        program, mesh=mesh, in_specs=in_specs, out_specs=out_specs, check_vma=False
    )
```

```python
import functools

import jax
import jax.numpy as jnp
from jax import lax
from jax.experimental import pallas as pl
from jax.experimental.pallas import tpu as pltpu
from jax.sharding import PartitionSpec as P

epsilon = 1e-05
score_scale = 0.015625
residual_scale = 0.22
rope_base = 10000000.0
masked_score = -1e30
key_block = 1024
score_chunk = 256
value_chunk = 256
token_tile = 128
prepare_pages = 8


def matmul(a, b):
    return jnp.dot(a, b, preferred_element_type=jnp.float32)


def vmem():
    return pl.BlockSpec(memory_space=pltpu.VMEM)


def anywhere():
    return pl.BlockSpec(memory_space=pl.ANY)


def smem():
    return pl.BlockSpec(memory_space=pltpu.SMEM)


def params(mebibytes):
    return pltpu.CompilerParams(vmem_limit_bytes=mebibytes * 1024 * 1024)


def cycle_tables(count):
    depth = count // 4
    walk = [(z, 0) for z in range(depth)] + [(z, 1) for z in reversed(range(depth))]
    device = lambda chip, core: (chip[0] * 2 + chip[1]) * 2 + core
    length = len(walk)
    ahead = [
        (device(walk[k], c), device(walk[(k + 1) % length], c))
        for k in range(length)
        for c in range(2)
    ]
    back = [(b, a) for a, b in ahead]
    swap = [(i, i ^ 1) for i in range(count)]
    order = [None] * count
    for k in range(length):
        for c in range(2):
            row = []
            for step in range(length // 2):
                sources = [walk[(k - step) % length], walk[(k + step) % length]]
                for chip in sources[: 1 if step == 0 else 2]:
                    row += [device(chip, c), device(chip, 1 - c)]
            far = walk[(k + length // 2) % length]
            row += [device(far, c), device(far, 1 - c)]
            order[device(walk[k], c)] = row
    return ahead, back, swap, order


def after(value, *others):
    return lax.optimization_barrier((value,) + others)[0]


def assemble_kernel(*refs):
    *blocks, out_ref, sems = refs
    rows = blocks[0].shape[0]
    copies = [
        pltpu.make_async_copy(block, out_ref.at[pl.ds(k * rows, rows)], sems.at[k])
        for k, block in enumerate(blocks)
    ]
    for copy in copies:
        copy.start()
    for copy in copies:
        copy.wait()


def assemble(blocks):
    rows, columns = blocks[0].shape
    return pl.pallas_call(
        assemble_kernel,
        in_specs=[anywhere()] * len(blocks),
        out_specs=vmem(),
        out_shape=jax.ShapeDtypeStruct((len(blocks) * rows, columns), blocks[0].dtype),
        scratch_shapes=[pltpu.SemaphoreType.DMA((len(blocks),))],
        cost_estimate=pl.CostEstimate(
            flops=0, bytes_accessed=4 * len(blocks) * rows * columns, transcendentals=0
        ),
        compiler_params=params(60),
        name="assemble",
    )(*blocks)


class Ring:
    def __init__(self, shard, tables):
        self.ahead, self.back, self.swap, self.order = tables
        self.up = self.down = shard
        self.blocks = [shard]

    def move(self, value, pairs):
        return lax.ppermute(value, "req", pairs)

    def step(self, *others):
        if others:
            self.up, self.down = lax.optimization_barrier((self.up, self.down) + others)[:2]
        self.up, self.down = self.move(self.up, self.ahead), self.move(self.down, self.back)
        self.blocks += [self.up, self.down]

    def last(self, upward, *others):
        if others:
            self.up, self.down = lax.optimization_barrier((self.up, self.down) + others)[:2]
        return self.move(self.up, self.ahead) if upward else self.move(self.down, self.back)

    def partner(self, *others):
        blocks = self.blocks
        if others:
            blocks = list(lax.optimization_barrier(tuple(blocks) + others)[: len(blocks)])
        return self.move(assemble(blocks), self.swap)

    def all(self, end, partner):
        return self.blocks + [end, partner, self.move(end, self.swap)]


def chunk_sources(refs):
    *own, partner, end = refs
    rows = own[0].shape[0]
    sources = []
    for k, block in enumerate(own):
        at = partner.at[pl.ds(k * rows, rows)] if k < len(own) - 1 else end
        sources += [block, at]
    return sources


def prepare_kernel(heads, page, width, pages_step, first_page, aliased, table_ref, length_ref, *refs):
    pages = refs[:pages_step]
    key_ref, value_ref, wide = refs[pages_step + aliased :]
    step = pl.program_id(0)
    half = width // 2
    rows = value_ref.shape[1]
    pick_row = lax.broadcasted_iota(jnp.int32, (rows, width), 0)
    pick_lane = lax.broadcasted_iota(jnp.int32, (rows, width), 1)
    pick = jnp.where(pick_lane == pick_row + half, 1.0, 0.0).astype(jnp.bfloat16)
    ones = jnp.where(lax.broadcasted_iota(jnp.int32, (rows, page), 0) == half, 1.0, 0.0)
    for i in range(pages_step):
        wide[i] = pages[i][0].astype(jnp.float32)
        first = (first_page + step * pages_step + i) * page
        position = first + lax.broadcasted_iota(jnp.int32, (page, width), 0)
        lane = lax.broadcasted_iota(jnp.int32, (page, width), 1)
        bias = jnp.where((lane == half) & (position >= length_ref[0]), masked_score, 0.0)
        for h in range(heads):
            rows_h = wide[i, pl.ds(h, page, stride=heads), :]
            key_ref[h, pl.ds(i * page, page), :] = jnp.where(lane < half, rows_h, bias).astype(
                jnp.bfloat16
            )
            turned = lax.dot_general(
                pick,
                rows_h.astype(jnp.bfloat16),
                (((1,), (1,)), ((), ())),
                preferred_element_type=jnp.float32,
            )
            value_ref[h, :, pl.ds(i * page, page)] = (turned + ones).astype(jnp.bfloat16)


def with_ones(turned):
    row = lax.broadcasted_iota(jnp.int32, (16, turned.shape[1]), 0)
    return jnp.concatenate([turned, jnp.where(row == 0, 1.0, 0.0)], axis=0)


def prepare(cache, table, length, part, parts, before):
    pages, page, heads, width = cache.shape
    pages_step = prepare_pages
    rows = width // 2 + 16
    total = table.shape[0]
    steps = total // pages_step // parts
    flat = cache.reshape(pages, page * heads, width)
    at = part * steps
    page_spec = lambda i: pl.BlockSpec(
        (1, page * heads, width), lambda j, t, n: (t[(at + j) * pages_step + i], 0, 0)
    )
    kept = [pl.BlockSpec(memory_space=pl.ANY)] * len(before)
    return pl.pallas_call(
        functools.partial(
            prepare_kernel, heads, page, width, pages_step, at * pages_step, len(before)
        ),
        grid_spec=pltpu.PrefetchScalarGridSpec(
            num_scalar_prefetch=2,
            grid=(steps,),
            in_specs=[page_spec(i) for i in range(pages_step)] + kept,
            out_specs=[
                pl.BlockSpec((heads, pages_step * page, width), lambda j, t, n: (0, at + j, 0)),
                pl.BlockSpec((heads, rows, pages_step * page), lambda j, t, n: (0, 0, at + j)),
            ],
            scratch_shapes=[pltpu.VMEM((pages_step, page * heads, width), jnp.float32)],
        ),
        out_shape=[
            jax.ShapeDtypeStruct((heads, total * page, width), jnp.bfloat16),
            jax.ShapeDtypeStruct((heads, rows, total * page), jnp.bfloat16),
        ],
        input_output_aliases={2 + pages_step + i: i for i in range(len(before))},
        cost_estimate=pl.CostEstimate(
            flops=0,
            bytes_accessed=3 * cache.size * cache.dtype.itemsize // parts,
            transcendentals=0,
        ),
        compiler_params=params(60),
        name="prepare",
    )(table, length, *([flat] * pages_step), *before)


def turn(pair, cosine, sines):
    half = pair.shape[0] // 2
    first, second = pair[:half], pair[half:]
    return jnp.concatenate(
        [first * cosine - second * sines, second * cosine + first * sines], axis=0
    )


def project_kernel(heads, new_heads, group, dim, blocks, device_ref, order_ref, *refs):
    device = device_ref[0]
    chunks = refs[:blocks]
    normed_hbm, cos_ref, sin_ref, query_ref = refs[blocks : blocks + 4]
    source, normed_ref, sems = refs[-3:]
    sources = chunks if blocks == 1 else chunk_sources(chunks)
    count = len(sources)
    rows = source.shape[0] // count
    copies = [pltpu.make_async_copy(normed_hbm, normed_ref, sems.at[count])]
    for k in range(count):
        start = pl.multiple_of(order_ref[device, k] * rows, rows)
        copies.append(pltpu.make_async_copy(sources[k], source.at[pl.ds(start, rows)], sems.at[k]))
    for copy in copies:
        copy.start()
    cosine, sines = cos_ref[...], sin_ref[...]
    tokens = cosine.shape[1]
    width = group * dim
    for copy in copies:
        copy.wait()
    normed = normed_ref[...]
    row = lax.broadcasted_iota(jnp.int32, (dim, group * token_tile), 0)
    one_row = jnp.where(row == 0, 1.0, 0.0).astype(jnp.bfloat16)
    for h in range(heads):
        turned = jnp.transpose(matmul(normed, source[:, pl.ds(h * width, width)]))
        for g in range(group):
            rotated = turn(turned[g * dim : (g + 1) * dim], cosine, sines).astype(jnp.bfloat16)
            scaled = (rotated.astype(jnp.float32) * score_scale).astype(jnp.bfloat16)
            for q in range(tokens // token_tile):
                query_ref[h, q, pl.ds(0, dim), pl.ds(g * token_tile, token_tile)] = scaled[
                    :, q * token_tile : (q + 1) * token_tile
                ]
        for q in range(tokens // token_tile):
            query_ref[h, q, pl.ds(dim, dim), :] = one_row
    for h in range(new_heads):
        key_ref, value_ref = refs[blocks + 4 : blocks + 6]
        at = heads * width + h * 2 * dim
        turned = jnp.transpose(matmul(normed, source[:, pl.ds(at, 2 * dim)]))
        keys = turn(turned[:dim], cosine, sines)
        padded = jnp.concatenate([keys, jnp.zeros_like(keys)], axis=0)
        key_ref[h] = jnp.transpose(padded).astype(jnp.bfloat16)
        value_ref[h] = with_ones(turned[dim:]).astype(jnp.bfloat16)


def project(normed, chunks, device, order, cosine, sines, heads, new_heads, group, dim):
    tokens, width = normed.shape
    columns = chunks[0].shape[1]
    outs = [(heads, tokens // token_tile, 2 * dim, group * token_tile)]
    if new_heads:
        outs += [(new_heads, tokens, 2 * dim), (new_heads, dim + 16, tokens)]
    return pl.pallas_call(
        functools.partial(project_kernel, heads, new_heads, group, dim, len(chunks)),
        in_specs=[smem()] * 2 + [anywhere()] * (len(chunks) + 1) + [vmem()] * 2,
        out_specs=[vmem()] * len(outs),
        out_shape=[jax.ShapeDtypeStruct(shape, jnp.bfloat16) for shape in outs],
        scratch_shapes=[
            pltpu.VMEM((width, columns), jnp.bfloat16),
            pltpu.VMEM((tokens, width), jnp.bfloat16),
            pltpu.SemaphoreType.DMA((order.shape[1] + 1,)),
        ],
        cost_estimate=pl.CostEstimate(
            flops=2 * tokens * width * columns,
            bytes_accessed=2 * width * columns,
            transcendentals=0,
        ),
        compiler_params=params(60),
        name="project",
    )(device, order, *chunks, normed, cosine, sines)


def column_max(scores):
    return jnp.max(scores.reshape(scores.shape[0] // 8, 8, scores.shape[1]), axis=0)


def attend_kernel(
    heads,
    first_query,
    first_head,
    length_ref,
    span_ref,
    tile_ref,
    keys_hbm,
    values_hbm,
    queries_hbm,
    out_ref,
    token_ref,
    even,
    odd,
    keys_ref,
    values_ref,
    queries_ref,
    key_sems,
    value_sems,
    query_sems,
):
    lanes = out_ref.shape[2]
    length = length_ref[0]
    token_ref[0] = length
    q = tile_ref[0]
    pair = 2 * key_block
    sum_row = values_hbm.shape[1] - 16
    live = q * token_tile < span_ref[0]
    pairs = jnp.where(live, (length + pair - 1) // pair, 0)
    last_block = jnp.maximum(2 * pairs - 1, 0)
    row = lax.broadcasted_iota(jnp.int32, out_ref.shape[1:], 0)

    def key_copy(h, i):
        piece = pl.ds(pl.multiple_of(i * pair, pair), pair)
        return pltpu.make_async_copy(
            keys_hbm.at[first_head + h, piece], keys_ref.at[h & 1, piece], key_sems.at[h & 1, i]
        )

    def value_copy(h, i):
        piece = pl.ds(pl.multiple_of(i * pair, pair), pair)
        return pltpu.make_async_copy(
            values_hbm.at[first_head + h, :, piece],
            values_ref.at[h & 1, :, piece],
            value_sems.at[h & 1, i],
        )

    def query_copy(h):
        return pltpu.make_async_copy(
            queries_hbm.at[first_query + h, q], queries_ref.at[h], query_sems.at[h]
        )

    def fetch(h):
        def one(i, _):
            key_copy(h, i).start()
            value_copy(h, i).start()
            return 0

        lax.fori_loop(0, pairs, one, 0)

    def attend_head(h, _):
        query_copy(h).wait()
        key_copy(h, 0).wait()

        @pl.when(h + 1 < heads)
        def ahead():
            fetch(h + 1)

        key_ref, value_ref, query_ref = keys_ref.at[h & 1], values_ref.at[h & 1], queries_ref.at[h]
        def scores_of(block, c, target):
            start = pl.multiple_of(block * key_block + c * score_chunk, score_chunk)
            scores = matmul(key_ref[pl.ds(start, score_chunk), :], query_ref[...])
            target[pl.ds(c * score_chunk, score_chunk), :] = scores
            return column_max(scores)

        def half(block, following, current, target, state):
            maximum, top, total = state
            new_maximum = jnp.maximum(maximum, jnp.max(top, axis=0, keepdims=True))
            total = total * jnp.exp(maximum - new_maximum)
            next_top = None
            ratio = value_chunk // score_chunk
            parts = []
            for c in range(key_block // score_chunk):
                seen = scores_of(following, c, target)
                next_top = seen if next_top is None else jnp.maximum(next_top, seen)
                part = jnp.exp(current[pl.ds(c * score_chunk, score_chunk), :] - new_maximum)
                parts.append(part.astype(jnp.bfloat16))
                if len(parts) == ratio:
                    weights = parts[0] if ratio == 1 else jnp.concatenate(parts, axis=0)
                    start = block * key_block + (c + 1 - ratio) * score_chunk
                    start = pl.multiple_of(start, value_chunk)
                    total = total + matmul(value_ref[:, pl.ds(start, value_chunk)], weights)
                    parts = []
            return new_maximum, next_top, total

        def advance(i, state):
            @pl.when(i + 1 < pairs)
            def arrived():
                key_copy(h, i + 1).wait()

            value_copy(h, i).wait()
            block = 2 * i
            state = half(block, block + 1, even, odd, state)
            following = jnp.minimum(block + 2, last_block)
            return half(block + 1, following, odd, even, state)

        top = scores_of(0, 0, even)
        for c in range(1, key_block // score_chunk):
            top = jnp.maximum(top, scores_of(0, c, even))
        start = (
            jnp.full((1, lanes), masked_score, jnp.float32),
            top,
            jnp.zeros(row.shape, jnp.float32),
        )
        maximum, _, total = lax.fori_loop(0, pairs, advance, start)
        out_ref[h] = jnp.where(row == sum_row + 1, maximum, total)
        return 0

    @pl.when(pairs > 0)
    def work():
        for h in range(heads):
            query_copy(h).start()
        fetch(0)
        lax.fori_loop(0, heads, attend_head, 0)

    @pl.when(pairs == 0)
    def nothing():
        for h in range(heads):
            out_ref[h] = jnp.where(row == sum_row + 1, masked_score, 0.0)


def attend(heads, first_query, first_head, tile, keys, values, queries, token, valid):
    _, cached, width = keys.shape
    rows = values.shape[1]
    lanes = queries.shape[3]
    pieces = cached // (2 * key_block)
    return pl.pallas_call(
        functools.partial(attend_kernel, heads, first_query, first_head),
        in_specs=[smem()] * 3 + [anywhere()] * 3,
        out_specs=[vmem(), smem()],
        out_shape=[
            jax.ShapeDtypeStruct((heads, rows, lanes), jnp.float32),
            jax.ShapeDtypeStruct((1,), jnp.int32),
        ],
        scratch_shapes=[pltpu.VMEM((key_block, lanes), jnp.float32)] * 2
        + [
            pltpu.VMEM((2, cached, width), jnp.bfloat16),
            pltpu.VMEM((2, rows, cached), jnp.bfloat16),
            pltpu.VMEM((heads, width, lanes), jnp.bfloat16),
            pltpu.SemaphoreType.DMA((2, pieces)),
            pltpu.SemaphoreType.DMA((2, pieces)),
            pltpu.SemaphoreType.DMA((heads,)),
        ],
        cost_estimate=pl.CostEstimate(
            flops=8 * heads * cached * lanes * 2 * width,
            bytes_accessed=2 * heads * cached * 2 * width,
            transcendentals=heads * cached * lanes,
        ),
        compiler_params=params(60),
        name="attend",
    )(token, valid, tile, keys, values, queries)


def finish_head(q, valid, group, dim, state, query, new_key, new_value):
    lanes = query.shape[1]
    span = new_key.shape[0]
    scores = matmul(new_key, query)
    source = lax.broadcasted_iota(jnp.int32, (span, lanes), 0)
    lane = lax.broadcasted_iota(jnp.int32, (span, lanes), 1)
    position = q * token_tile + lax.rem(lane, token_tile)
    scores = jnp.where((source <= position) & (source < valid), scores, masked_score)
    cached_maximum = state[dim + 1 : dim + 2]
    maximum = jnp.maximum(jnp.max(column_max(scores), axis=0, keepdims=True), cached_maximum)
    weights = jnp.exp(scores - maximum).astype(jnp.bfloat16)
    total = state * jnp.exp(cached_maximum - maximum) + matmul(new_value, weights)
    result = total[:dim] / total[dim : dim + 1]
    row = q * token_tile + lax.broadcasted_iota(jnp.int32, (token_tile, 2 * dim), 0)
    pieces = []
    for g in range(0, group, 2):
        both = jnp.concatenate(
            [
                result[:, g * token_tile : (g + 1) * token_tile],
                result[:, (g + 1) * token_tile : (g + 2) * token_tile],
            ],
            axis=0,
        )
        pieces.append(jnp.where(row < valid, jnp.transpose(both), 0.0).astype(jnp.bfloat16))
    return pieces


def finish_kernel(heads, sets, group, dim, blocks, final, span_ref, tile_ref, *refs):
    if final:
        device_ref, order_ref, other_hbm, *refs = refs
        *refs, other, other_sem = refs
    states_hbm = refs[:sets]
    queries_hbm = refs[sets : sets + len(heads)]
    new_keys_hbm, new_values_hbm = refs[sets + len(heads) : sets + len(heads) + 2]
    at = sets + len(heads) + 2
    chunks = refs[at : at + blocks]
    out_ref, token_ref = refs[at + blocks : at + blocks + 2]
    states, queries, new_keys, new_values, weight, sems, weight_sems = refs[at + blocks + 2 :]
    q = tile_ref[0]
    token_ref[0] = q
    total = sum(heads)
    per_set = total // sets
    chunks = chunk_sources(chunks) if blocks else []
    count = len(chunks)
    columns = weight.shape[2]
    copies = []
    for i in range(sets):
        copies.append((states_hbm[i], states.at[pl.ds(i * per_set, per_set)]))
    copies += [(new_keys_hbm, new_keys), (new_values_hbm, new_values)]
    source = [(which, h) for which, count in enumerate(heads) for h in range(count)]
    for h in range(total):
        which, place = source[h]
        copies.append((queries_hbm[which].at[place, q], queries.at[h]))
    copies = [pltpu.make_async_copy(a, b, sems.at[i]) for i, (a, b) in enumerate(copies)]
    loads = [
        pltpu.make_async_copy(
            chunks[k], weight.at[k], weight_sems.at[k]
        )
        for k in range(count)
    ]
    if final:
        loads.append(pltpu.make_async_copy(other_hbm, other, other_sem))
    for copy in copies + loads:
        copy.start()
    for copy in copies:
        copy.wait()
    pieces = []
    for h in range(total):
        pieces += finish_head(
            q, span_ref[0], group, dim, states[h], queries[h], new_keys[h], new_values[h]
        )
    attended = jnp.concatenate(pieces, axis=1)
    if blocks == 0:
        out_ref[...] = attended
        return
    for copy in loads:
        copy.wait()
    for k in range(0, count, 2):
        wide = jnp.concatenate([weight[k], weight[k + 1]], axis=1)
        both = matmul(attended, wide).astype(jnp.bfloat16)
        for i in range(2):
            term = both[:, i * columns : (i + 1) * columns]
            if final:
                summed = term.astype(jnp.float32) + other[k + i].astype(jnp.float32)
                start = pl.multiple_of(order_ref[device_ref[0], k + i] * columns, columns)
                out_ref[:, pl.ds(start, columns)] = (residual_scale * summed).astype(jnp.bfloat16)
            else:
                out_ref[k + i] = term


def finish(states, tile, valid, queries, new_keys, new_values, group, chunks, final=()):
    heads = tuple(q.shape[0] for q in queries)
    total = sum(heads)
    rows, lanes = states[0].shape[1:]
    dim = rows - 16
    depth = total * group * dim
    blocks = len(chunks)
    count = 2 * (blocks - 2) if blocks else 0
    columns = chunks[0].shape[1] if blocks else 128
    out = (count, token_tile, columns) if blocks else (token_tile, depth)
    landing = []
    if final:
        out = (token_tile, count * columns)
        landing = [pltpu.VMEM(final[2].shape, jnp.bfloat16), pltpu.SemaphoreType.DMA(())]
    return pl.pallas_call(
        functools.partial(finish_kernel, heads, len(states), group, dim, blocks, bool(final)),
        in_specs=[smem()] * 2
        + ([smem(), smem(), anywhere()] if final else [])
        + [anywhere()] * (len(states) + len(queries) + 2 + blocks),
        out_specs=[vmem(), smem()],
        out_shape=[
            jax.ShapeDtypeStruct(out, jnp.bfloat16),
            jax.ShapeDtypeStruct((1,), jnp.int32),
        ],
        scratch_shapes=[
            pltpu.VMEM((total, rows, lanes), jnp.float32),
            pltpu.VMEM((total,) + queries[0].shape[2:], jnp.bfloat16),
            pltpu.VMEM(new_keys.shape, jnp.bfloat16),
            pltpu.VMEM(new_values.shape, jnp.bfloat16),
            pltpu.VMEM((max(count, 1), depth if blocks else 16, columns), jnp.bfloat16),
            pltpu.SemaphoreType.DMA((len(states) + 2 + total,)),
            pltpu.SemaphoreType.DMA((max(count, 1),)),
        ]
        + landing,
        cost_estimate=pl.CostEstimate(
            flops=2 * token_tile * depth * columns * count,
            bytes_accessed=2 * depth * columns * count,
            transcendentals=0,
        ),
        compiler_params=params(60),
        name="finish",
    )(valid, tile, *final, *states, *queries, new_keys, new_values, *chunks)


def rope_tables(positions, dim):
    half_dim = dim // 2
    frequency = rope_base ** (-(jnp.arange(half_dim, dtype=jnp.float32) * 2.0 / dim))
    angles = positions.astype(jnp.float32)[None, :] * frequency[:, None]
    return jnp.cos(angles), jnp.sin(angles)


def body(req_count, tp_count, tokens, norm_gain, w_query, w_kv, w_out, kv_cache, page_table, cached_len, span_len):
    fast = tp_count == 2 and req_count == 16 and w_out.shape[1] % 128 == 0 and w_kv.shape[1] == 4
    device = lax.axis_index("req")
    rank = lax.axis_index("tp")
    heads = w_kv.shape[1]
    dim = w_kv.shape[2] // 2
    group = w_query.shape[1] // dim // heads
    own_rows = tokens.shape[0]
    length = jnp.sum(
        jnp.where(jnp.arange(cached_len.shape[0]) == device, cached_len, 0), keepdims=True
    )
    table = page_table[0]
    w_new = w_kv.reshape(w_kv.shape[0], -1)
    if fast:
        tables = cycle_tables(req_count)
        order = jnp.array(tables[3], jnp.int32)
        place = device.reshape(1)
        swap = [(0, 1), (1, 0)]
        early = heads // 2
        cut = early * group * dim
        ring_first = Ring(w_query[:, :cut], tables)
        ring_second = Ring(jnp.concatenate([w_query[:, cut:], w_new], axis=1), tables)
        ring_out = Ring(w_out, tables)
        other = lax.ppermute(tokens, "tp", swap)
        whole = jnp.concatenate(
            [jnp.where(rank == 0, tokens, other), jnp.where(rank == 0, other, tokens)], axis=0
        )
        parts = 2
        state = ()
        ring_first.step()
        ring_second.step()
        for part in range(parts):
            state = prepare(kv_cache, table, length, part, parts, state)
            ring_first.step()
            ring_second.step(state[0])
        first_end = ring_first.last(True)
        first_chunks = ring_first.all(first_end, ring_first.partner())
        ring_out.step(first_end)
        keys, values = state
    else:
        order = jnp.zeros((1, 1), jnp.int32)
        place = jnp.zeros((1,), jnp.int32)
        early = 0
        gather = lambda array: lax.all_gather(array, "req", axis=0, tiled=True)
        second_chunks = [gather(jnp.concatenate([w_query, w_new], axis=1))]
        whole = lax.all_gather(tokens, "tp", axis=0, tiled=True)
        keys, values = prepare(kv_cache, table, length, 0, 1, ())
    hidden = whole.astype(jnp.float32)
    normed = (
        hidden * lax.rsqrt(jnp.mean(hidden * hidden, axis=-1, keepdims=True) + epsilon) * norm_gain
    ).astype(jnp.bfloat16)
    positions = length[0] + jnp.arange(normed.shape[0], dtype=jnp.int32)
    cosine, sines = rope_tables(positions, dim)
    queries = []

    def attend_tile(tile, source, count, first, token):
        return attend(count, 0, first, tile, keys, values, source, token, span_len)

    def finish_tile(states, tile, chunks, final=()):
        return finish(states, tile, span_len, queries, new_keys, new_values, group, chunks, final)

    if not fast:
        late, new_keys, new_values = project(
            normed, second_chunks, place, order, cosine, sines, heads, heads, group, dim
        )
        queries.append(late)
        rows = []
        for q in range(normed.shape[0] // token_tile):
            tile = jnp.full((1,), q, jnp.int32)
            state, _ = attend_tile(tile, late, heads, 0, length)
            rows.append(finish_tile([state], tile, [])[0])
        gathered = lax.all_gather(w_out, "req", axis=1, tiled=True)
        partial = matmul(jnp.concatenate(rows, axis=0), gathered).astype(jnp.bfloat16)
        summed = lax.psum_scatter(partial, "tp", scatter_dimension=0, tiled=True)
        return (residual_scale * summed.astype(jnp.float32)).astype(jnp.bfloat16)
    theirs, ours = (1 - rank).reshape(1), rank.reshape(1)
    soon = project(normed, first_chunks, place, order, cosine, sines, early, 0, group, dim)[0]
    second_end = ring_second.last(False, soon)
    ring_out.step(soon)
    sent_first, token = attend_tile(theirs, soon, early, 0, length)
    second_chunks = ring_second.all(after(second_end, sent_first), ring_second.partner(sent_first))
    ring_out.step(sent_first)
    kept_first, token = attend_tile(ours, soon, early, 0, token)
    late, new_keys, new_values = project(
        normed, second_chunks, place, order, cosine, sines, heads - early, heads, group, dim
    )
    queries += [soon, late]
    out_end = ring_out.last(True, kept_first)
    out_partner = ring_out.partner(kept_first)
    sent_second, token = attend_tile(theirs, late, heads - early, early, token)
    out_chunks = ring_out.all(after(out_end, sent_second), out_partner)
    sent, tile_token = finish_tile([sent_first, sent_second], theirs, out_chunks)
    received = lax.ppermute(sent, "tp", swap)
    token = token + (tile_token - theirs)
    kept_second, token = attend_tile(ours, late, heads - early, early, token)
    final = (place, order, received)
    return finish_tile([kept_first, kept_second], ours, out_chunks, final)[0]


def solution(mesh):
    in_specs = (
        P(("req", "tp"), None),
        P(),
        P("req", "tp"),
        P("req", "tp", None),
        P("tp", "req"),
        P("req", None, "tp", None),
        P("req", None),
        P(),
        P("req"),
    )
    out_specs = P(("req", "tp"), None)
    program = functools.partial(body, mesh.shape["req"], mesh.shape["tp"])
    return jax.shard_map(
        program, mesh=mesh, in_specs=in_specs, out_specs=out_specs, check_vma=False
    )
```

```python
import functools

import jax
import jax.numpy as jnp
from jax import lax
from jax.experimental import pallas as pl
from jax.experimental.pallas import tpu as pltpu
from jax.sharding import PartitionSpec as P

epsilon = 1e-05
score_scale = 0.015625
residual_scale = 0.22
rope_base = 10000000.0
masked_score = -1e30
key_block = 1024
score_chunk = 256
value_chunk = 256
token_tile = 128
prepare_pages = 8


def matmul(a, b):
    return jnp.dot(a, b, preferred_element_type=jnp.float32)


def vmem():
    return pl.BlockSpec(memory_space=pltpu.VMEM)


def anywhere():
    return pl.BlockSpec(memory_space=pl.ANY)


def smem():
    return pl.BlockSpec(memory_space=pltpu.SMEM)


def params(mebibytes):
    return pltpu.CompilerParams(vmem_limit_bytes=mebibytes * 1024 * 1024)


def cycle_tables(count):
    depth = count // 4
    walk = [(z, 0) for z in range(depth)] + [(z, 1) for z in reversed(range(depth))]
    device = lambda chip, core: (chip[0] * 2 + chip[1]) * 2 + core
    length = len(walk)
    ahead = [
        (device(walk[k], c), device(walk[(k + 1) % length], c))
        for k in range(length)
        for c in range(2)
    ]
    back = [(b, a) for a, b in ahead]
    swap = [(i, i ^ 1) for i in range(count)]
    order = [None] * count
    for k in range(length):
        for c in range(2):
            row = []
            for step in range(length // 2):
                sources = [walk[(k - step) % length], walk[(k + step) % length]]
                for chip in sources[: 1 if step == 0 else 2]:
                    row += [device(chip, c), device(chip, 1 - c)]
            far = walk[(k + length // 2) % length]
            row += [device(far, c), device(far, 1 - c)]
            order[device(walk[k], c)] = row
    return ahead, back, swap, order


def after(value, *others):
    return lax.optimization_barrier((value,) + others)[0]


def assemble_kernel(*refs):
    *blocks, out_ref, sems = refs
    rows = blocks[0].shape[0]
    copies = [
        pltpu.make_async_copy(block, out_ref.at[pl.ds(k * rows, rows)], sems.at[k])
        for k, block in enumerate(blocks)
    ]
    for copy in copies:
        copy.start()
    for copy in copies:
        copy.wait()


def assemble(blocks):
    rows, columns = blocks[0].shape
    return pl.pallas_call(
        assemble_kernel,
        in_specs=[anywhere()] * len(blocks),
        out_specs=vmem(),
        out_shape=jax.ShapeDtypeStruct((len(blocks) * rows, columns), blocks[0].dtype),
        scratch_shapes=[pltpu.SemaphoreType.DMA((len(blocks),))],
        cost_estimate=pl.CostEstimate(
            flops=0, bytes_accessed=4 * len(blocks) * rows * columns, transcendentals=0
        ),
        compiler_params=params(60),
        name="assemble",
    )(*blocks)


class Ring:
    def __init__(self, shard, tables):
        self.ahead, self.back, self.swap, self.order = tables
        self.up = self.down = shard
        self.blocks = [shard]

    def move(self, value, pairs):
        return lax.ppermute(value, "req", pairs)

    def step(self, *others):
        if others:
            self.up, self.down = lax.optimization_barrier((self.up, self.down) + others)[:2]
        self.up, self.down = self.move(self.up, self.ahead), self.move(self.down, self.back)
        self.blocks += [self.up, self.down]

    def last(self, upward, *others):
        if others:
            self.up, self.down = lax.optimization_barrier((self.up, self.down) + others)[:2]
        return self.move(self.up, self.ahead) if upward else self.move(self.down, self.back)

    def partner(self, *others):
        blocks = self.blocks
        if others:
            blocks = list(lax.optimization_barrier(tuple(blocks) + others)[: len(blocks)])
        return self.move(assemble(blocks), self.swap)

    def all(self, end, partner):
        return self.blocks + [end, partner, self.move(end, self.swap)]


def chunk_sources(refs):
    *own, partner, end = refs
    rows = own[0].shape[0]
    sources = []
    for k, block in enumerate(own):
        at = partner.at[pl.ds(k * rows, rows)] if k < len(own) - 1 else end
        sources += [block, at]
    return sources


def prepare_kernel(heads, page, width, pages_step, first_page, aliased, table_ref, length_ref, *refs):
    pages = refs[:pages_step]
    key_ref, value_ref, wide = refs[pages_step + aliased :]
    step = pl.program_id(0)
    half = width // 2
    for i in range(pages_step):
        wide[i] = pages[i][0].astype(jnp.float32)
        first = (first_page + step * pages_step + i) * page
        position = first + lax.broadcasted_iota(jnp.int32, (page, width), 0)
        lane = lax.broadcasted_iota(jnp.int32, (page, width), 1)
        bias = jnp.where((lane == half) & (position >= length_ref[0]), masked_score, 0.0)
        for h in range(heads):
            rows_h = wide[i, pl.ds(h, page, stride=heads), :]
            key_ref[h, pl.ds(i * page, page), :] = jnp.where(lane < half, rows_h, bias).astype(
                jnp.bfloat16
            )
            turned = with_ones(jnp.transpose(rows_h)[half:])
            value_ref[h, :, pl.ds(i * page, page)] = turned.astype(jnp.bfloat16)


def with_ones(turned):
    row = lax.broadcasted_iota(jnp.int32, (16, turned.shape[1]), 0)
    return jnp.concatenate([turned, jnp.where(row == 0, 1.0, 0.0)], axis=0)


def prepare(cache, table, length, part, parts, before):
    pages, page, heads, width = cache.shape
    pages_step = prepare_pages
    rows = width // 2 + 16
    total = table.shape[0]
    steps = total // pages_step // parts
    flat = cache.reshape(pages, page * heads, width)
    at = part * steps
    page_spec = lambda i: pl.BlockSpec(
        (1, page * heads, width), lambda j, t, n: (t[(at + j) * pages_step + i], 0, 0)
    )
    kept = [pl.BlockSpec(memory_space=pl.ANY)] * len(before)
    return pl.pallas_call(
        functools.partial(
            prepare_kernel, heads, page, width, pages_step, at * pages_step, len(before)
        ),
        grid_spec=pltpu.PrefetchScalarGridSpec(
            num_scalar_prefetch=2,
            grid=(steps,),
            in_specs=[page_spec(i) for i in range(pages_step)] + kept,
            out_specs=[
                pl.BlockSpec((heads, pages_step * page, width), lambda j, t, n: (0, at + j, 0)),
                pl.BlockSpec((heads, rows, pages_step * page), lambda j, t, n: (0, 0, at + j)),
            ],
            scratch_shapes=[pltpu.VMEM((pages_step, page * heads, width), jnp.float32)],
        ),
        out_shape=[
            jax.ShapeDtypeStruct((heads, total * page, width), jnp.bfloat16),
            jax.ShapeDtypeStruct((heads, rows, total * page), jnp.bfloat16),
        ],
        input_output_aliases={2 + pages_step + i: i for i in range(len(before))},
        cost_estimate=pl.CostEstimate(
            flops=0,
            bytes_accessed=3 * cache.size * cache.dtype.itemsize // parts,
            transcendentals=0,
        ),
        compiler_params=params(60),
        name="prepare",
    )(table, length, *([flat] * pages_step), *before)


def turn(pair, cosine, sines):
    half = pair.shape[0] // 2
    first, second = pair[:half], pair[half:]
    return jnp.concatenate(
        [first * cosine - second * sines, second * cosine + first * sines], axis=0
    )


def project_kernel(heads, new_heads, group, dim, blocks, fresh, device_ref, order_ref, *refs):
    device = device_ref[0]
    if fresh:
        rank_ref, gain_ref, own_hbm, other_hbm, *refs = refs
        *refs, fresh_sems = refs
    chunks = refs[:blocks]
    if fresh:
        cos_ref, sin_ref, query_ref, normed_out = refs[blocks : blocks + 4]
    else:
        normed_hbm, cos_ref, sin_ref, query_ref = refs[blocks : blocks + 4]
    source, normed_ref, sems = refs[-3:]
    sources = chunks if blocks == 1 else chunk_sources(chunks)
    count = len(sources)
    rows = source.shape[0] // count
    if fresh:
        size = own_hbm.shape[0]
        first = pl.ds(pl.multiple_of(rank_ref[0] * size, size), size)
        second = pl.ds(pl.multiple_of((1 - rank_ref[0]) * size, size), size)
        copies = [
            pltpu.make_async_copy(own_hbm, normed_ref.at[first], fresh_sems.at[0]),
            pltpu.make_async_copy(other_hbm, normed_ref.at[second], fresh_sems.at[1]),
        ]
    else:
        copies = [pltpu.make_async_copy(normed_hbm, normed_ref, sems.at[count])]
    for k in range(count):
        start = pl.multiple_of(order_ref[device, k] * rows, rows)
        copies.append(pltpu.make_async_copy(sources[k], source.at[pl.ds(start, rows)], sems.at[k]))
    for copy in copies:
        copy.start()
    cosine, sines = cos_ref[...], sin_ref[...]
    tokens = cosine.shape[1]
    width = group * dim
    if fresh:
        for copy in copies[:2]:
            copy.wait()
        hidden = normed_ref[...].astype(jnp.float32)
        scale = lax.rsqrt(jnp.mean(hidden * hidden, axis=-1, keepdims=True) + epsilon)
        normed = (hidden * scale * gain_ref[...]).astype(jnp.bfloat16)
        normed_out[...] = normed
        normed_ref[...] = normed
        copies = copies[2:]
    for copy in copies:
        copy.wait()
    normed = normed_ref[...]
    row = lax.broadcasted_iota(jnp.int32, (dim, group * token_tile), 0)
    one_row = jnp.where(row == 0, 1.0, 0.0).astype(jnp.bfloat16)
    for h in range(heads):
        turned = jnp.transpose(matmul(normed, source[:, pl.ds(h * width, width)]))
        for g in range(group):
            rotated = turn(turned[g * dim : (g + 1) * dim], cosine, sines).astype(jnp.bfloat16)
            scaled = (rotated.astype(jnp.float32) * score_scale).astype(jnp.bfloat16)
            for q in range(tokens // token_tile):
                query_ref[h, q, pl.ds(0, dim), pl.ds(g * token_tile, token_tile)] = scaled[
                    :, q * token_tile : (q + 1) * token_tile
                ]
        for q in range(tokens // token_tile):
            query_ref[h, q, pl.ds(dim, dim), :] = one_row
    for h in range(new_heads):
        key_ref, value_ref = refs[blocks + 4 : blocks + 6]
        at = heads * width + h * 2 * dim
        turned = jnp.transpose(matmul(normed, source[:, pl.ds(at, 2 * dim)]))
        keys = turn(turned[:dim], cosine, sines)
        padded = jnp.concatenate([keys, jnp.zeros_like(keys)], axis=0)
        key_ref[h] = jnp.transpose(padded).astype(jnp.bfloat16)
        value_ref[h] = with_ones(turned[dim:]).astype(jnp.bfloat16)


def project(normed, chunks, device, order, cosine, sines, heads, new_heads, group, dim):
    fresh = isinstance(normed, tuple)
    inputs = [*normed[2:], *chunks] if fresh else [*chunks, normed]
    scalars = list(normed[:2]) if fresh else []
    tokens, width = (2 * normed[2].shape[0], normed[2].shape[1]) if fresh else normed.shape
    columns = chunks[0].shape[1]
    outs = [(heads, tokens // token_tile, 2 * dim, group * token_tile)]
    if new_heads:
        outs += [(new_heads, tokens, 2 * dim), (new_heads, dim + 16, tokens)]
    if fresh:
        outs.append((tokens, width))
    return pl.pallas_call(
        functools.partial(project_kernel, heads, new_heads, group, dim, len(chunks), fresh),
        in_specs=[smem()] * 2
        + ([smem(), vmem()] if fresh else [])
        + [anywhere()] * len(inputs)
        + [vmem()] * 2,
        out_specs=[vmem()] * len(outs),
        out_shape=[jax.ShapeDtypeStruct(shape, jnp.bfloat16) for shape in outs],
        scratch_shapes=[
            pltpu.VMEM((width, columns), jnp.bfloat16),
            pltpu.VMEM((tokens, width), jnp.bfloat16),
            pltpu.SemaphoreType.DMA((order.shape[1] + 1,)),
        ]
        + ([pltpu.SemaphoreType.DMA((2,))] if fresh else []),
        cost_estimate=pl.CostEstimate(
            flops=2 * tokens * width * columns,
            bytes_accessed=2 * width * columns,
            transcendentals=0,
        ),
        compiler_params=params(60),
        name="project",
    )(device, order, *scalars, *inputs, cosine, sines)


def column_max(scores):
    return jnp.max(scores.reshape(scores.shape[0] // 8, 8, scores.shape[1]), axis=0)


def attend_kernel(
    heads,
    first_query,
    first_head,
    length_ref,
    span_ref,
    tile_ref,
    keys_hbm,
    values_hbm,
    queries_hbm,
    out_ref,
    token_ref,
    even,
    odd,
    keys_ref,
    values_ref,
    queries_ref,
    key_sems,
    value_sems,
    query_sems,
):
    lanes = out_ref.shape[2]
    length = length_ref[0]
    token_ref[0] = length
    q = tile_ref[0]
    pair = 2 * key_block
    sum_row = values_hbm.shape[1] - 16
    live = q * token_tile < span_ref[0]
    pairs = jnp.where(live, (length + pair - 1) // pair, 0)
    last_block = jnp.maximum(2 * pairs - 1, 0)
    row = lax.broadcasted_iota(jnp.int32, out_ref.shape[1:], 0)

    def key_copy(h, i):
        piece = pl.ds(pl.multiple_of(i * pair, pair), pair)
        return pltpu.make_async_copy(
            keys_hbm.at[first_head + h, piece], keys_ref.at[h & 1, piece], key_sems.at[h & 1, i]
        )

    def value_copy(h, i):
        piece = pl.ds(pl.multiple_of(i * pair, pair), pair)
        return pltpu.make_async_copy(
            values_hbm.at[first_head + h, :, piece],
            values_ref.at[h & 1, :, piece],
            value_sems.at[h & 1, i],
        )

    def query_copy(h):
        return pltpu.make_async_copy(
            queries_hbm.at[first_query + h, q], queries_ref.at[h], query_sems.at[h]
        )

    def fetch(h):
        def one(i, _):
            key_copy(h, i).start()
            value_copy(h, i).start()
            return 0

        lax.fori_loop(0, pairs, one, 0)

    def attend_head(h, _):
        query_copy(h).wait()
        key_copy(h, 0).wait()

        @pl.when(h + 1 < heads)
        def ahead():
            fetch(h + 1)

        key_ref, value_ref, query_ref = keys_ref.at[h & 1], values_ref.at[h & 1], queries_ref.at[h]
        def scores_of(block, c, target):
            start = pl.multiple_of(block * key_block + c * score_chunk, score_chunk)
            scores = matmul(key_ref[pl.ds(start, score_chunk), :], query_ref[...])
            target[pl.ds(c * score_chunk, score_chunk), :] = scores
            return column_max(scores)

        def half(block, following, current, target, state):
            maximum, top, total = state
            new_maximum = jnp.maximum(maximum, jnp.max(top, axis=0, keepdims=True))
            total = total * jnp.exp(maximum - new_maximum)
            next_top = None
            ratio = value_chunk // score_chunk
            parts = []
            for c in range(key_block // score_chunk):
                seen = scores_of(following, c, target)
                next_top = seen if next_top is None else jnp.maximum(next_top, seen)
                part = jnp.exp(current[pl.ds(c * score_chunk, score_chunk), :] - new_maximum)
                parts.append(part.astype(jnp.bfloat16))
                if len(parts) == ratio:
                    weights = parts[0] if ratio == 1 else jnp.concatenate(parts, axis=0)
                    start = block * key_block + (c + 1 - ratio) * score_chunk
                    start = pl.multiple_of(start, value_chunk)
                    total = total + matmul(value_ref[:, pl.ds(start, value_chunk)], weights)
                    parts = []
            return new_maximum, next_top, total

        def advance(i, state):
            @pl.when(i + 1 < pairs)
            def arrived():
                key_copy(h, i + 1).wait()

            value_copy(h, i).wait()
            block = 2 * i
            state = half(block, block + 1, even, odd, state)
            following = jnp.minimum(block + 2, last_block)
            return half(block + 1, following, odd, even, state)

        top = scores_of(0, 0, even)
        for c in range(1, key_block // score_chunk):
            top = jnp.maximum(top, scores_of(0, c, even))
        start = (
            jnp.full((1, lanes), masked_score, jnp.float32),
            top,
            jnp.zeros(row.shape, jnp.float32),
        )
        maximum, _, total = lax.fori_loop(0, pairs, advance, start)
        out_ref[h] = jnp.where(row == sum_row + 1, maximum, total)
        return 0

    @pl.when(pairs > 0)
    def work():
        for h in range(heads):
            query_copy(h).start()
        fetch(0)
        lax.fori_loop(0, heads, attend_head, 0)

    @pl.when(pairs == 0)
    def nothing():
        for h in range(heads):
            out_ref[h] = jnp.where(row == sum_row + 1, masked_score, 0.0)


def attend(heads, first_query, first_head, tile, keys, values, queries, token, valid):
    _, cached, width = keys.shape
    rows = values.shape[1]
    lanes = queries.shape[3]
    pieces = cached // (2 * key_block)
    return pl.pallas_call(
        functools.partial(attend_kernel, heads, first_query, first_head),
        in_specs=[smem()] * 3 + [anywhere()] * 3,
        out_specs=[vmem(), smem()],
        out_shape=[
            jax.ShapeDtypeStruct((heads, rows, lanes), jnp.float32),
            jax.ShapeDtypeStruct((1,), jnp.int32),
        ],
        scratch_shapes=[pltpu.VMEM((key_block, lanes), jnp.float32)] * 2
        + [
            pltpu.VMEM((2, cached, width), jnp.bfloat16),
            pltpu.VMEM((2, rows, cached), jnp.bfloat16),
            pltpu.VMEM((heads, width, lanes), jnp.bfloat16),
            pltpu.SemaphoreType.DMA((2, pieces)),
            pltpu.SemaphoreType.DMA((2, pieces)),
            pltpu.SemaphoreType.DMA((heads,)),
        ],
        cost_estimate=pl.CostEstimate(
            flops=8 * heads * cached * lanes * 2 * width,
            bytes_accessed=2 * heads * cached * 2 * width,
            transcendentals=heads * cached * lanes,
        ),
        compiler_params=params(60),
        name="attend",
    )(token, valid, tile, keys, values, queries)


def finish_head(q, valid, group, dim, state, query, new_key, new_value):
    lanes = query.shape[1]
    span = new_key.shape[0]
    scores = matmul(new_key, query)
    source = lax.broadcasted_iota(jnp.int32, (span, lanes), 0)
    lane = lax.broadcasted_iota(jnp.int32, (span, lanes), 1)
    position = q * token_tile + lax.rem(lane, token_tile)
    scores = jnp.where((source <= position) & (source < valid), scores, masked_score)
    cached_maximum = state[dim + 1 : dim + 2]
    maximum = jnp.maximum(jnp.max(column_max(scores), axis=0, keepdims=True), cached_maximum)
    weights = jnp.exp(scores - maximum).astype(jnp.bfloat16)
    total = state * jnp.exp(cached_maximum - maximum) + matmul(new_value, weights)
    result = total[:dim] / total[dim : dim + 1]
    row = q * token_tile + lax.broadcasted_iota(jnp.int32, (token_tile, 2 * dim), 0)
    pieces = []
    for g in range(0, group, 2):
        both = jnp.concatenate(
            [
                result[:, g * token_tile : (g + 1) * token_tile],
                result[:, (g + 1) * token_tile : (g + 2) * token_tile],
            ],
            axis=0,
        )
        pieces.append(jnp.where(row < valid, jnp.transpose(both), 0.0).astype(jnp.bfloat16))
    return pieces


def finish_kernel(heads, sets, group, dim, blocks, final, span_ref, tile_ref, *refs):
    if final:
        device_ref, order_ref, other_hbm, *refs = refs
        *refs, other, other_sem = refs
    states_hbm = refs[:sets]
    queries_hbm = refs[sets : sets + len(heads)]
    new_keys_hbm, new_values_hbm = refs[sets + len(heads) : sets + len(heads) + 2]
    at = sets + len(heads) + 2
    chunks = refs[at : at + blocks]
    out_ref, token_ref = refs[at + blocks : at + blocks + 2]
    states, queries, new_keys, new_values, weight, sems, weight_sems = refs[at + blocks + 2 :]
    q = tile_ref[0]
    token_ref[0] = q
    total = sum(heads)
    per_set = total // sets
    chunks = chunk_sources(chunks) if blocks else []
    count = len(chunks)
    columns = weight.shape[2]
    copies = []
    for i in range(sets):
        copies.append((states_hbm[i], states.at[pl.ds(i * per_set, per_set)]))
    copies += [(new_keys_hbm, new_keys), (new_values_hbm, new_values)]
    source = [(which, h) for which, count in enumerate(heads) for h in range(count)]
    for h in range(total):
        which, place = source[h]
        copies.append((queries_hbm[which].at[place, q], queries.at[h]))
    copies = [pltpu.make_async_copy(a, b, sems.at[i]) for i, (a, b) in enumerate(copies)]
    loads = [
        pltpu.make_async_copy(
            chunks[k], weight.at[k], weight_sems.at[k]
        )
        for k in range(count)
    ]
    if final:
        loads.append(pltpu.make_async_copy(other_hbm, other, other_sem))
    for copy in copies + loads:
        copy.start()
    for copy in copies:
        copy.wait()
    pieces = []
    for h in range(total):
        pieces += finish_head(
            q, span_ref[0], group, dim, states[h], queries[h], new_keys[h], new_values[h]
        )
    attended = jnp.concatenate(pieces, axis=1)
    if blocks == 0:
        out_ref[...] = attended
        return
    for copy in loads:
        copy.wait()
    for k in range(0, count, 2):
        wide = jnp.concatenate([weight[k], weight[k + 1]], axis=1)
        both = matmul(attended, wide).astype(jnp.bfloat16)
        for i in range(2):
            term = both[:, i * columns : (i + 1) * columns]
            if final:
                summed = term.astype(jnp.float32) + other[k + i].astype(jnp.float32)
                start = pl.multiple_of(order_ref[device_ref[0], k + i] * columns, columns)
                out_ref[:, pl.ds(start, columns)] = (residual_scale * summed).astype(jnp.bfloat16)
            else:
                out_ref[k + i] = term


def finish(states, tile, valid, queries, new_keys, new_values, group, chunks, final=()):
    heads = tuple(q.shape[0] for q in queries)
    total = sum(heads)
    rows, lanes = states[0].shape[1:]
    dim = rows - 16
    depth = total * group * dim
    blocks = len(chunks)
    count = 2 * (blocks - 2) if blocks else 0
    columns = chunks[0].shape[1] if blocks else 128
    out = (count, token_tile, columns) if blocks else (token_tile, depth)
    landing = []
    if final:
        out = (token_tile, count * columns)
        landing = [pltpu.VMEM(final[2].shape, jnp.bfloat16), pltpu.SemaphoreType.DMA(())]
    return pl.pallas_call(
        functools.partial(finish_kernel, heads, len(states), group, dim, blocks, bool(final)),
        in_specs=[smem()] * 2
        + ([smem(), smem(), anywhere()] if final else [])
        + [anywhere()] * (len(states) + len(queries) + 2 + blocks),
        out_specs=[vmem(), smem()],
        out_shape=[
            jax.ShapeDtypeStruct(out, jnp.bfloat16),
            jax.ShapeDtypeStruct((1,), jnp.int32),
        ],
        scratch_shapes=[
            pltpu.VMEM((total, rows, lanes), jnp.float32),
            pltpu.VMEM((total,) + queries[0].shape[2:], jnp.bfloat16),
            pltpu.VMEM(new_keys.shape, jnp.bfloat16),
            pltpu.VMEM(new_values.shape, jnp.bfloat16),
            pltpu.VMEM((max(count, 1), depth if blocks else 16, columns), jnp.bfloat16),
            pltpu.SemaphoreType.DMA((len(states) + 2 + total,)),
            pltpu.SemaphoreType.DMA((max(count, 1),)),
        ]
        + landing,
        cost_estimate=pl.CostEstimate(
            flops=2 * token_tile * depth * columns * count,
            bytes_accessed=2 * depth * columns * count,
            transcendentals=0,
        ),
        compiler_params=params(60),
        name="finish",
    )(valid, tile, *final, *states, *queries, new_keys, new_values, *chunks)


def rope_tables(positions, dim):
    half_dim = dim // 2
    frequency = rope_base ** (-(jnp.arange(half_dim, dtype=jnp.float32) * 2.0 / dim))
    angles = positions.astype(jnp.float32)[None, :] * frequency[:, None]
    return jnp.cos(angles), jnp.sin(angles)


def body(req_count, tp_count, tokens, norm_gain, w_query, w_kv, w_out, kv_cache, page_table, cached_len, span_len):
    fast = tp_count == 2 and req_count == 16 and w_out.shape[1] % 128 == 0 and w_kv.shape[1] == 4
    device = lax.axis_index("req")
    rank = lax.axis_index("tp")
    heads = w_kv.shape[1]
    dim = w_kv.shape[2] // 2
    group = w_query.shape[1] // dim // heads
    own_rows = tokens.shape[0]
    length = jnp.sum(
        jnp.where(jnp.arange(cached_len.shape[0]) == device, cached_len, 0), keepdims=True
    )
    table = page_table[0]
    w_new = w_kv.reshape(w_kv.shape[0], -1)
    if fast:
        tables = cycle_tables(req_count)
        order = jnp.array(tables[3], jnp.int32)
        place = device.reshape(1)
        swap = [(0, 1), (1, 0)]
        early = heads // 2
        cut = early * group * dim
        ring_first = Ring(w_query[:, :cut], tables)
        ring_second = Ring(jnp.concatenate([w_query[:, cut:], w_new], axis=1), tables)
        ring_out = Ring(w_out, tables)
        other = lax.ppermute(tokens, "tp", swap)
        parts = 2
        state = ()
        ring_first.step()
        ring_second.step()
        for part in range(parts):
            state = prepare(kv_cache, table, length, part, parts, state)
            ring_first.step()
            ring_second.step(state[0])
        first_end = ring_first.last(True)
        first_chunks = ring_first.all(first_end, ring_first.partner())
        ring_out.step(first_end)
        keys, values = state
    else:
        order = jnp.zeros((1, 1), jnp.int32)
        place = jnp.zeros((1,), jnp.int32)
        early = 0
        gather = lambda array: lax.all_gather(array, "req", axis=0, tiled=True)
        second_chunks = [gather(jnp.concatenate([w_query, w_new], axis=1))]
        whole = lax.all_gather(tokens, "tp", axis=0, tiled=True)
        keys, values = prepare(kv_cache, table, length, 0, 1, ())
    if not fast:
        hidden = whole.astype(jnp.float32)
        normed = (
            hidden * lax.rsqrt(jnp.mean(hidden * hidden, axis=-1, keepdims=True) + epsilon) * norm_gain
        ).astype(jnp.bfloat16)
    positions = length[0] + jnp.arange(tp_count * own_rows, dtype=jnp.int32)
    cosine, sines = rope_tables(positions, dim)
    queries = []

    def attend_tile(tile, source, count, first, token):
        return attend(count, 0, first, tile, keys, values, source, token, span_len)

    def finish_tile(states, tile, chunks, final=()):
        return finish(states, tile, span_len, queries, new_keys, new_values, group, chunks, final)

    if not fast:
        late, new_keys, new_values = project(
            normed, second_chunks, place, order, cosine, sines, heads, heads, group, dim
        )
        queries.append(late)
        rows = []
        for q in range(normed.shape[0] // token_tile):
            tile = jnp.full((1,), q, jnp.int32)
            state, _ = attend_tile(tile, late, heads, 0, length)
            rows.append(finish_tile([state], tile, [])[0])
        gathered = lax.all_gather(w_out, "req", axis=1, tiled=True)
        partial = matmul(jnp.concatenate(rows, axis=0), gathered).astype(jnp.bfloat16)
        summed = lax.psum_scatter(partial, "tp", scatter_dimension=0, tiled=True)
        return (residual_scale * summed.astype(jnp.float32)).astype(jnp.bfloat16)
    theirs, ours = (1 - rank).reshape(1), rank.reshape(1)
    fresh = (rank.reshape(1), norm_gain.reshape(1, -1), tokens, other)
    soon, normed = project(
        fresh, first_chunks, place, order, cosine, sines, early, 0, group, dim
    )
    second_end = ring_second.last(False, soon)
    ring_out.step(soon)
    sent_first, token = attend_tile(theirs, soon, early, 0, length)
    second_chunks = ring_second.all(after(second_end, sent_first), ring_second.partner(sent_first))
    ring_out.step(sent_first)
    kept_first, token = attend_tile(ours, soon, early, 0, token)
    late, new_keys, new_values = project(
        normed, second_chunks, place, order, cosine, sines, heads - early, heads, group, dim
    )
    queries += [soon, late]
    out_end = ring_out.last(True, kept_first)
    out_partner = ring_out.partner(kept_first)
    sent_second, token = attend_tile(theirs, late, heads - early, early, token)
    out_chunks = ring_out.all(after(out_end, sent_second), out_partner)
    sent, tile_token = finish_tile([sent_first, sent_second], theirs, out_chunks)
    received = lax.ppermute(sent, "tp", swap)
    token = token + (tile_token - theirs)
    kept_second, token = attend_tile(ours, late, heads - early, early, token)
    final = (place, order, received)
    return finish_tile([kept_first, kept_second], ours, out_chunks, final)[0]


def solution(mesh):
    in_specs = (
        P(("req", "tp"), None),
        P(),
        P("req", "tp"),
        P("req", "tp", None),
        P("tp", "req"),
        P("req", None, "tp", None),
        P("req", None),
        P(),
        P("req"),
    )
    out_specs = P(("req", "tp"), None)
    program = functools.partial(body, mesh.shape["req"], mesh.shape["tp"])
    return jax.shard_map(
        program, mesh=mesh, in_specs=in_specs, out_specs=out_specs, check_vma=False
    )
```
